32 devices in a mesh: dev: 32 (over z, y, x, core).
Axes of the slice: x: 2, y: 2, z: 4, core: 2. Of those that a mesh axis runs over, the one named last changes fastest.
Arguments:
- tokens: bfloat16 [10240, 1600], P('dev'), may hold values from -6 to 6
- cotangent: bfloat16 [10240, 1600], P('dev'), may hold values from -6 to 6
- w_qkv: bfloat16 [38400, 200], P('dev')
- w_out: bfloat16 [12800, 200], P('dev'), may hold values from -0.625 to 0.625
- w_fc: bfloat16 [51200, 200], P('dev'), may hold values from -0.15625 to 0.15625
- w_proj: bfloat16 [51200, 200], P('dev'), may hold values from -0.078125 to 0.078125
- ln1_gain: float32 [1600], replicated, may hold values from 0.5 to 1.5
- ln1_bias: float32 [1600], replicated, may hold values from -1.25 to 1.25
- q_bias: float32 [1600], replicated, may hold values from -1.75 to 1.75
- v_bias: float32 [1600], replicated, may hold values from -1.75 to 1.75
- out_bias: float32 [1600], replicated, may hold values from -1.75 to 1.75
- ln2_gain: float32 [1600], replicated, may hold values from 0.5 to 1.5
- ln2_bias: float32 [1600], replicated, may hold values from -1.25 to 1.25
- fc_bias: float32 [6400], replicated, may hold values from -1.75 to 1.75
- proj_bias: float32 [1600], replicated, may hold values from -1.75 to 1.75
- seg_lengths: int32 [4, 13], replicated, may hold values from 1 to 1024, 2560 in all within a row
- parents: int32 [4, 13], replicated, may hold values from 0 to 11, as said below
Outputs:
- output: bfloat16 [10240, 1600], P('dev')
- input_grad: float32 [10240, 1600], P('dev')
- qkv_grad: float32 [38400, 200], P('dev')
- out_grad: float32 [12800, 200], P('dev')
- fc_grad: float32 [51200, 200], P('dev')
- proj_grad: float32 [51200, 200], P('dev')
- ln1_gain_grad: float32 [1600], replicated
- ln1_bias_grad: float32 [1600], replicated
- q_bias_grad: float32 [1600], replicated
- v_bias_grad: float32 [1600], replicated
- out_bias_grad: float32 [1600], replicated
- ln2_gain_grad: float32 [1600], replicated
- ln2_bias_grad: float32 [1600], replicated
- fc_bias_grad: float32 [6400], replicated
- proj_bias_grad: float32 [1600], replicated
- logit_max: float32 [25], replicated
- clipped_qkv: bfloat16 [38400, 200], P('dev')
The draws below stay inside these ranges and needn't reach their ends.
Inputs may be any that keep to these rules, and one draw needn't show every extreme that they name: `seg_lengths`: the 13 lengths of a tree sum to 2560. parents[t, 0] is 0 and marks the root; for s >= 1, parents[t, s] < s.
All inputs are finite; a program needn't handle non-finite values.
Results may differ from the reference program's by a relative error of at most 0.013.
The reference program's roundings to bfloat16 on the way count: a program that leaves them out, or rounds other values in their place, can miss the bound.
Values may be sent and summed in bfloat16 or wider, within the bound.
No kernel may reach another device: no remote copies, remote signals or barrier semaphores. Data moves between devices by JAX's collectives and lax.ppermute only.
A program may use at most 448 MiB of HBM per device.

```python
import math
from functools import partial
import jax
import jax.numpy as jnp
import numpy as np
from jax import lax

D = 1600
FF = 6400
HEAD_DIM = 64
FLAT = 200
SEGS = 13
TREE_TOK = 2560
TOKENS = 10240
TREES = 4


def draw_w_qkv(key, part):
    row_count = 3 * D * D // FLAT
    base_key, head_key = jax.random.split(jax.random.fold_in(key, 11))
    base = jax.random.normal(base_key, (row_count, FLAT), jnp.float32)
    head_count = D // HEAD_DIM
    lift = jnp.exp(jax.random.uniform(head_key, (head_count,), jnp.float32, math.log(0.7), math.log(2.5)))
    flat_index = jnp.arange(row_count * FLAT, dtype=jnp.int32).reshape(row_count, FLAT)
    column = flat_index % (3 * D)
    head_of = column % D // HEAD_DIM
    factor = jnp.where(column < D, lift[head_of], 1.0)
    return (base * factor * D ** (-0.5)).astype(jnp.bfloat16)


def draw_parents(key, part):
    numbers = jnp.arange(SEGS, dtype=jnp.int32)
    raw_bits = jax.random.randint(jax.random.fold_in(key, 23), (TREES, SEGS), 0, 1 << 20)
    chosen = raw_bits % jnp.maximum(numbers[None, :], 1)
    picked_tree = jax.random.randint(jax.random.fold_in(key, 29), (), 0, TREES)
    tree_numbers = jnp.arange(TREES, dtype=jnp.int32)
    forced = (tree_numbers[:, None] == picked_tree) & (numbers[None, :] == SEGS - 1)
    chosen = jnp.where(forced, SEGS - 2, chosen)
    return jnp.where(numbers[None, :] > 0, chosen, 0).astype(jnp.int32)


def block_levels(stream_key, dims, cuts, least, top_value):
    loudness = 1.0
    for dim, blocks in cuts:
        draws = jax.random.uniform(jax.random.fold_in(jax.random.fold_in(stream_key, 6), dim), (blocks,), jnp.float32, least / len(cuts), top_value / len(cuts))
        loudness = loudness * jnp.repeat(jnp.exp(draws), dims[dim] // blocks).reshape((-1,) + (1,) * (len(dims) - 1 - dim))
    return loudness


def split_up(amount, total, most, skew):
    loads = [(1 << 20) // math.isqrt(rank ** skew) + 1 for rank in range(2, amount + 1)]
    rest, given = total - most - (amount - 1), [1] * (amount - 1)
    while rest > 0:
        free = [i for i in range(amount - 1) if given[i] < most]
        whole, left = sum([loads[i] for i in free]), rest
        for i in free:
            addition = min(most - given[i], max(1, left * loads[i] // whole), rest)
            given[i] = given[i] + addition
            rest = rest - addition
    return np.array([most] + given)


def ragged_sizes(stream_key, count, total, bound, lean):
    if count == 2:
        one = jax.random.randint(stream_key, (), max(1, total - bound), min(bound, total - 1) + 1)
        return jnp.stack([one, total - one])
    sizes = jnp.asarray(split_up(count, total, bound, lean), jnp.int32)
    pairs = (count - 1) // 2
    donor, taker = sizes[1:1 + 2 * pairs:2], sizes[2:2 + 2 * pairs:2]
    slack = jnp.minimum(donor - 1, bound - taker)
    shifted = jax.random.randint(jax.random.fold_in(stream_key, 1), (pairs,), 0, 1 << 20) % (slack + 1)
    sizes = sizes.at[1:1 + 2 * pairs:2].set(donor - shifted).at[2:2 + 2 * pairs:2].set(taker + shifted)
    return sizes[jax.random.permutation(jax.random.fold_in(stream_key, 2), count)]


def normal_values(own_key, shape, scale, bound, pieces=(), kind=jnp.bfloat16):
    factor_of = block_levels(own_key, shape, pieces, -0.22, 0.18) if pieces else 1.0
    array = jax.random.normal(own_key, shape, jnp.float32) * scale * factor_of
    return jnp.minimum(jnp.maximum(array, -bound), bound).astype(kind)


def setup_inputs(seed: int = 0) -> dict:
    arg_keys = jax.random.split(jax.random.key(seed), 18)
    tokens = normal_values(arg_keys[0], (TOKENS, D), 1.0, 6.0, ((0, 32),))
    cotangent = normal_values(arg_keys[1], (TOKENS, D), 1.0, 6.0, ((0, 32),))
    w_qkv = draw_w_qkv(jax.random.fold_in(arg_keys[17], 71), 0)
    w_out = normal_values(arg_keys[3], (D * D // FLAT, FLAT), (D // 16) ** -0.5, 0.625, ((0, 32),))
    w_fc = normal_values(arg_keys[4], (D * FF // FLAT, FLAT), D ** -0.5, 0.15625, ((0, 32),))
    w_proj = normal_values(arg_keys[5], (FF * D // FLAT, FLAT), FF ** -0.5, 0.078125, ((0, 32),))
    ln1_gain = jnp.clip(1.0 + 0.1 * jax.random.normal(arg_keys[6], (D,), jnp.float32), 0.5, 1.5)
    ln1_bias = normal_values(arg_keys[7], (D,), 0.2, 1.25, (), jnp.float32)
    q_bias = normal_values(arg_keys[8], (D,), 0.3, 1.75, (), jnp.float32)
    v_bias = normal_values(arg_keys[9], (D,), 0.3, 1.75, (), jnp.float32)
    out_bias = normal_values(arg_keys[10], (D,), 0.3, 1.75, (), jnp.float32)
    ln2_gain = jnp.clip(1.0 + 0.1 * jax.random.normal(arg_keys[11], (D,), jnp.float32), 0.5, 1.5)
    ln2_bias = normal_values(arg_keys[12], (D,), 0.2, 1.25, (), jnp.float32)
    fc_bias = normal_values(arg_keys[13], (FF,), 0.3, 1.75, (), jnp.float32)
    proj_bias = normal_values(arg_keys[14], (D,), 0.3, 1.75, (), jnp.float32)
    seg_lengths = jax.vmap(lambda own: ragged_sizes(own, SEGS, TREE_TOK, TREE_TOK * 2 // 5, 1))(jax.random.split(arg_keys[15], TREES)).reshape((TREES, SEGS)).astype(jnp.int32)
    parents = draw_parents(jax.random.fold_in(arg_keys[17], 71), 0)
    return {"tokens": tokens, "cotangent": cotangent, "w_qkv": w_qkv, "w_out": w_out, "w_fc": w_fc, "w_proj": w_proj, "ln1_gain": ln1_gain, "ln1_bias": ln1_bias, "q_bias": q_bias, "v_bias": v_bias, "out_bias": out_bias, "ln2_gain": ln2_gain, "ln2_bias": ln2_bias, "fc_bias": fc_bias, "proj_bias": proj_bias, "seg_lengths": seg_lengths, "parents": parents}


EPS = 1e-05
TAU = 7.0
HIGH = lax.Precision.HIGHEST

@jax.custom_vjp
def low(v):
    return lax.optimization_barrier(v.astype(jnp.bfloat16)).astype(jnp.float32)

@jax.custom_vjp
def low_back(v):
    return v

def low_keep(v):
    return (low(v), None)

def low_pass(kept, grad):
    return (grad,)

def back_keep(v):
    return (v, None)

def back_low(kept, grad):
    return (low(grad),)
low.defvjp(low_keep, low_pass)
low_back.defvjp(back_keep, back_low)

def layer_norm(values, norm_gain, norm_shift):
    row_mean = lax.optimization_barrier(jnp.mean(values, axis=-1, keepdims=True))
    centered = values - row_mean
    variance = lax.optimization_barrier(jnp.mean(centered * centered, axis=-1, keepdims=True))
    return centered * lax.rsqrt(variance + EPS) * norm_gain + norm_shift

def tree_tables(lengths, parent_row):
    seg_count = lengths.shape[0]
    segment_ends = jnp.cumsum(lengths)
    numbers = jnp.arange(seg_count, dtype=jnp.int32)
    ancestry = numbers[:, None] == numbers[None, :]
    cursor = numbers
    for stride in range(seg_count - 1):
        cursor = parent_row[cursor]
        ancestry = ancestry | (cursor[:, None] == numbers[None, :])
    return (segment_ends, ancestry)

def tree_mask(lengths, parent_row, tree_size):
    segment_ends, ancestry = tree_tables(lengths, parent_row)
    position = jnp.arange(tree_size, dtype=jnp.int32)
    segment = lax.optimization_barrier(jnp.sum((position[:, None] >= segment_ends[None, :]).astype(jnp.int32), axis=1))
    linked = ancestry[segment][:, segment]
    return linked & (position[None, :] <= position[:, None])

def head_attention(allowed, parts):
    queries, key_rows, value_rows = (parts[0], parts[1], parts[2])
    score_scale = queries.shape[-1] ** (-0.5)
    raw = low_back(jnp.dot(queries, key_rows.T, precision=HIGH) * score_scale)
    masked = jnp.where(allowed, raw, -1e+30)
    probs = low(jax.nn.softmax(masked, axis=-1))
    return (jnp.dot(probs, value_rows, precision=HIGH), jnp.max(masked))

def forward(seg_lengths, parents, residual_in, w_qkv, w_out, w_fc, w_proj, ln1_gain, ln1_bias, q_bias, v_bias, out_bias, ln2_gain, ln2_bias, fc_bias, proj_bias):
    model_width = residual_in.shape[1]
    head_count = model_width // HEAD_DIM
    first_low = low(layer_norm(residual_in, ln1_gain, ln1_bias))
    qkv_bias = jnp.concatenate([q_bias, jnp.zeros_like(q_bias), v_bias])
    projected = low_back(low(jnp.dot(first_low, w_qkv, precision=HIGH) + qkv_bias))
    tree_count = seg_lengths.shape[0]
    per_tree = projected.reshape(tree_count, -1, 3, head_count, HEAD_DIM)

    def one_tree(item):
        block, lengths, parent_row = item
        tree_size = block.shape[0]
        allowed = tree_mask(lengths, parent_row, tree_size)
        stacked = jnp.transpose(block, (2, 1, 0, 3))
        attended, maxima = lax.map(jax.checkpoint(lambda parts: head_attention(allowed, parts)), stacked)
        return (jnp.transpose(attended, (1, 0, 2)).reshape(tree_size, model_width), maxima)
    attended, maxima = lax.map(one_tree, (per_tree, seg_lengths, parents))
    attn_low = low_back(low(attended.reshape(-1, model_width)))
    middle = residual_in + low_back(jnp.dot(attn_low, w_out, precision=HIGH) + out_bias)
    second_low = low(layer_norm(middle, ln2_gain, ln2_bias))
    pre_act = low_back(jnp.dot(second_low, w_fc, precision=HIGH) + fc_bias)
    act_low = low(jax.nn.gelu(pre_act, approximate=True))
    output = middle + low_back(jnp.dot(act_low, w_proj, precision=HIGH) + proj_bias)
    return (output, lax.optimization_barrier(jnp.max(maxima, axis=0)))

def reference(tokens, cotangent, w_qkv, w_out, w_fc, w_proj, ln1_gain, ln1_bias, q_bias, v_bias, out_bias, ln2_gain, ln2_bias, fc_bias, proj_bias, seg_lengths, parents):
    model_width = tokens.shape[1]
    hidden = fc_bias.shape[0]
    flat_cols = w_qkv.shape[1]
    primals = (tokens.astype(jnp.float32), w_qkv.astype(jnp.float32).reshape(model_width, 3 * model_width), w_out.astype(jnp.float32).reshape(model_width, model_width), w_fc.astype(jnp.float32).reshape(model_width, hidden), w_proj.astype(jnp.float32).reshape(hidden, model_width), ln1_gain, ln1_bias, q_bias, v_bias, out_bias, ln2_gain, ln2_bias, fc_bias, proj_bias)
    output, pullback, maxima = jax.vjp(partial(forward, seg_lengths, parents), *primals, has_aux=True)
    grads = pullback(cotangent.astype(jnp.float32))
    clip_gain = jnp.sqrt(TAU / jnp.maximum(maxima, TAU))
    column = jnp.arange(3 * model_width, dtype=jnp.int32)
    head_gain = clip_gain[column % model_width // HEAD_DIM]
    factor = jnp.where(column < 2 * model_width, head_gain, 1.0)
    clipped = (primals[1] * factor[None, :]).astype(jnp.bfloat16).reshape(-1, flat_cols)
    return (output.astype(jnp.bfloat16), grads[0], grads[1].reshape(-1, flat_cols), grads[2].reshape(-1, flat_cols), grads[3].reshape(-1, flat_cols), grads[4].reshape(-1, flat_cols), grads[5], grads[6], grads[7], grads[8], grads[9], grads[10], grads[11], grads[12], grads[13], maxima, clipped)
```

```python
from functools import partial

import jax
import jax.numpy as jnp
from jax import lax
from jax.experimental import pallas as pl
from jax.experimental.pallas import tpu as pltpu
from jax.sharding import Mesh, PartitionSpec as P

HEAD_DIM = 64
TREE_TOK = 2560
GROUP = 8

EPS = 1e-05
TAU = 7.0
NEGATIVE = -1e30

BQ = 256
BK = 256
LANES = 128

TREE = "t"
PLANE = ("a", "b", "c")
EVERY = ("t", "a", "b", "c")
BF = jnp.bfloat16
F32 = jnp.float32


def norm_forward(values, norm_gain, norm_shift):
    row_mean = jnp.mean(values, axis=-1, keepdims=True)
    centered = values - row_mean
    inv_std = lax.rsqrt(jnp.mean(centered * centered, axis=-1, keepdims=True) + EPS)
    normed = centered * inv_std
    return (normed * norm_gain + norm_shift, normed, inv_std)


def norm_backward(upstream, normed, inv_std, norm_gain):
    scaled = upstream * norm_gain
    inner = (
        scaled
        - jnp.mean(scaled, axis=-1, keepdims=True)
        - normed * jnp.mean(scaled * normed, axis=-1, keepdims=True)
    )
    return (inner * inv_std, jnp.sum(upstream * normed, axis=0), jnp.sum(upstream, axis=0))


def swap(value, axis):
    return lax.ppermute(value, axis, [(0, 1), (1, 0)])


def plane_gather(own):
    half = own.shape[0] // 2
    from_b, from_a = swap(own, "b"), swap(own, "a")
    diag = jnp.concatenate([swap(from_b[:half], "a"), swap(from_a[half:], "b")], axis=0)
    same = [own, from_b, from_a, diag]
    other = [swap(block, "c") for block in same]
    return [block for pair in zip(same, other) for block in pair]


def plane_scatter(part):
    sums = []
    for r in (6, 2, 4, 0):
        sums.append(part(r).astype(F32) + swap(part(r + 1), "c").astype(F32))
    diag, for_b, for_a, mine = sums
    half = diag.shape[0] // 2
    diag_low = diag.astype(BF)
    top = swap(diag_low[:half], "b")
    bottom = swap(diag_low[half:], "a")
    for_a = jnp.concatenate([for_a[:half] + top.astype(F32), for_a[half:]], axis=0)
    for_b = jnp.concatenate([for_b[:half], for_b[half:] + bottom.astype(F32)], axis=0)
    return (
        mine
        + swap(for_b.astype(BF), "b").astype(F32)
        + swap(for_a.astype(BF), "a").astype(F32)
    )


def block_of(array, index, rows):
    return lax.dynamic_slice_in_dim(array, index * rows, rows, 0)


def xor_order(array, place, rows):
    return jnp.concatenate([block_of(array, place ^ r, rows) for r in range(GROUP)], axis=0)


def tree_tables(lengths, parent_row):
    count = lengths.shape[0]
    numbers = jnp.arange(count, dtype=jnp.int32)
    ends = jnp.sum(jnp.where(numbers[None, :] <= numbers[:, None], lengths[None, :], 0), axis=1)
    starts = ends - lengths
    reach = (
        (numbers[:, None] == numbers[None, :]) | (parent_row[:, None] == numbers[None, :])
    ).astype(F32)
    hops = 1
    while hops < count:
        reach = (
            jnp.sum(reach[:, :, None] * reach[None, :, :], axis=1) > 0.5
        ).astype(F32)
        hops *= 2
    return starts, ends, reach


def block_lists(hot, path, q_blocks, k_blocks):
    q_has = jnp.max(path.reshape(q_blocks, -1, path.shape[1]), axis=1)
    k_has = jnp.max(hot.reshape(k_blocks, -1, hot.shape[1]), axis=1)
    live = jnp.sum(q_has[:, None, :] * k_has[None, :, :], axis=2) > 0.5
    q_first = jnp.arange(q_blocks, dtype=jnp.int32) * (BQ // BK)
    keys = jnp.arange(k_blocks, dtype=jnp.int32)
    live = (live & (keys[None, :] < q_first[:, None])).astype(jnp.int32)
    rank = jnp.sum(
        jnp.where(keys[None, :, None] > keys[None, None, :], live[:, None, :], 0), axis=2
    )
    listed = jnp.sum(
        jnp.where(
            (rank[:, :, None] == keys[None, None, :]) & (live[:, :, None] > 0),
            keys[None, :, None],
            0,
        ),
        axis=1,
    )
    return jnp.sum(live, axis=1).astype(jnp.int32), listed.astype(jnp.int32)


def score_block(kx, qx):
    return lax.dot_general(kx, qx, (((1,), (1,)), ((), ())), preferred_element_type=F32)


def causal(key_first, query_first):
    keys = key_first + lax.broadcasted_iota(jnp.int32, (BK, BQ), 0)
    queries = query_first + lax.broadcasted_iota(jnp.int32, (BK, BQ), 1)
    return keys <= queries


def attend_kernel(count, listed, owned, qx, kx, vt, out, out_wide, lse, top, m_s, l_s, acc_s):
    step = pl.program_id(0)
    q_first = step * BQ
    per = BQ // BK

    @pl.when(step == 0)
    def _():
        top[...] = jnp.full(top.shape, NEGATIVE, F32)

    def one(h, kb, diagonal):
        rows = pl.ds(pl.multiple_of(kb * BK, BK), BK)
        score = score_block(kx[h, rows, :], qx[h])
        if diagonal:
            score = jnp.where(causal(kb * BK, q_first), score, NEGATIVE)
        old = m_s[h : h + 1, :]
        new = jnp.maximum(old, jnp.max(score, axis=0, keepdims=True))
        weight = jnp.exp(score - new)
        shrink = jnp.exp(old - new)
        m_s[h : h + 1, :] = new
        l_s[h : h + 1, :] = l_s[h : h + 1, :] * shrink + jnp.sum(weight, axis=0, keepdims=True)
        acc_s[h] = acc_s[h] * shrink + jnp.dot(
            vt[h, :, rows], weight.astype(BF), preferred_element_type=F32
        )

    def heads(group):
        for h in group:
            m_s[h : h + 1, :] = jnp.full((1, BQ), NEGATIVE, F32)
            l_s[h : h + 1, :] = jnp.zeros((1, BQ), F32)
            acc_s[h] = jnp.zeros((HEAD_DIM, BQ), F32)
        for d in range(per):
            for h in group:
                one(h, step * per + d, True)

        def body(i, carry):
            for h in group:
                one(h, listed[step, i], False)
            return carry

        lax.fori_loop(0, count[step], body, 0)
        for h in group:
            total = l_s[h : h + 1, :]
            wide = acc_s[h] / total
            out_wide[h] = wide
            lse[h : h + 1, :] = m_s[h : h + 1, :] + jnp.log(total)
            top[h : h + 1, :] = jnp.maximum(top[h : h + 1, :], m_s[h : h + 1, :])

    last = acc_s.shape[0] - 1
    heads(range(last))

    @pl.when(owned[step] > 0)
    def _():
        heads([last])

    @pl.when(owned[step] == 0)
    def _():
        out_wide[last] = jnp.zeros((HEAD_DIM, BQ), F32)
        lse[last : last + 1, :] = jnp.zeros((1, BQ), F32)

    for h in range(last + 1):
        out[:, h * HEAD_DIM : (h + 1) * HEAD_DIM] = out_wide[h].T.astype(BF)


def attend(count, listed, owned, qx, kx, vt):
    heads, tokens, width = qx.shape
    steps = tokens // BQ
    spec = lambda shape, index: pl.BlockSpec(shape, index)
    whole = lambda shape: pl.BlockSpec(shape, lambda i, *_: (0,) * len(shape))
    return pl.pallas_call(
        attend_kernel,
        grid_spec=pltpu.PrefetchScalarGridSpec(
            num_scalar_prefetch=3,
            grid=(steps,),
            in_specs=[
                spec((heads, BQ, width), lambda i, *_: (0, i, 0)),
                whole(kx.shape),
                whole(vt.shape),
            ],
            out_specs=[
                spec((BQ, heads * HEAD_DIM), lambda i, *_: (i, 0)),
                spec((heads, HEAD_DIM, BQ), lambda i, *_: (0, 0, i)),
                spec((heads, BQ), lambda i, *_: (0, i)),
                whole((heads, BQ)),
            ],
            scratch_shapes=[
                pltpu.VMEM((heads, BQ), F32),
                pltpu.VMEM((heads, BQ), F32),
                pltpu.VMEM((heads, HEAD_DIM, BQ), F32),
            ],
        ),
        out_shape=[
            jax.ShapeDtypeStruct((tokens, heads * HEAD_DIM), BF),
            jax.ShapeDtypeStruct((heads, HEAD_DIM, tokens), F32),
            jax.ShapeDtypeStruct((heads, tokens), F32),
            jax.ShapeDtypeStruct((heads, BQ), F32),
        ],
        compiler_params=pltpu.CompilerParams(
            dimension_semantics=("arbitrary",), vmem_limit_bytes=48 << 20
        ),
        cost_estimate=pl.CostEstimate(
            flops=heads * tokens * tokens * HEAD_DIM * 4,
            bytes_accessed=heads * tokens * 1024,
            transcendentals=heads * tokens * tokens // 2,
        ),
        name="attend",
    )(count, listed, owned, qx, kx, vt)


def attend_back_kernel(
    count, listed, owned, qx, kx, kt, vs, up, out_wide, lse, grads, dk_s, dv_s, dq_s
):
    step = pl.program_id(0)
    q_first = step * BQ
    per = BQ // BK
    heads_all = dq_s.shape[0]
    last = heads_all - 1
    width = heads_all * HEAD_DIM

    @pl.when(step == 0)
    def _():
        dk_s[...] = jnp.zeros(dk_s.shape, F32)
        dv_s[...] = jnp.zeros(dv_s.shape, F32)

    def heads(group):
        parts = {}
        for h in group:
            rows_up = up[:, h * HEAD_DIM : (h + 1) * HEAD_DIM]
            cols_up = rows_up.astype(F32).T
            delta = jnp.sum(out_wide[h] * cols_up, axis=0, keepdims=True)
            parts[h] = (rows_up, cols_up.astype(BF), delta, lse[h : h + 1, :])
            dq_s[h] = jnp.zeros((HEAD_DIM, BQ), F32)

        def one(h, kb, diagonal):
            rows_up, cols_up, delta, norm = parts[h]
            rows = pl.ds(pl.multiple_of(kb * BK, BK), BK)
            score = score_block(kx[h, rows, :], qx[h])
            probs = jnp.exp(score - norm)
            if diagonal:
                probs = jnp.where(causal(kb * BK, q_first), probs, 0.0)
            dprobs = jnp.dot(vs[h, rows, :], cols_up, preferred_element_type=F32)
            dscore = (probs * (dprobs - delta)).astype(BF)
            dv_s[h, rows, :] += jnp.dot(probs.astype(BF), rows_up, preferred_element_type=F32)
            dk_s[h, rows, :] += jnp.dot(
                dscore, qx[h][:, :HEAD_DIM], preferred_element_type=F32
            )
            dq_s[h] += jnp.dot(kt[h, :, rows], dscore, preferred_element_type=F32)

        for d in range(per):
            for h in group:
                one(h, step * per + d, True)

        def body(i, carry):
            for h in group:
                one(h, listed[step, i], False)
            return carry

        lax.fori_loop(0, count[step], body, 0)

    heads(range(last))

    @pl.when(owned[step] > 0)
    def _():
        heads([last])

    @pl.when(owned[step] == 0)
    def _():
        dq_s[last] = jnp.zeros((HEAD_DIM, BQ), F32)

    here = pl.ds(pl.multiple_of(q_first, BQ), BQ)
    for h in range(heads_all):
        grads[here, h * HEAD_DIM : (h + 1) * HEAD_DIM] = (
            dq_s[h] * (HEAD_DIM ** (-0.5))
        ).T.astype(BF)

    @pl.when(step == pl.num_programs(0) - 1)
    def _():
        for h in range(heads_all):
            at = width + h * HEAD_DIM
            grads[:, at : at + HEAD_DIM] = dk_s[h].astype(BF)
            at = 2 * width + h * HEAD_DIM
            grads[:, at : at + HEAD_DIM] = dv_s[h].astype(BF)


def attend_back(count, listed, owned, qx, kx, kt, vs, up, out_wide, lse):
    heads, tokens, width = qx.shape
    steps = tokens // BQ
    spec = lambda shape, index: pl.BlockSpec(shape, index)
    whole = lambda shape: pl.BlockSpec(shape, lambda i, *_: (0,) * len(shape))
    return pl.pallas_call(
        attend_back_kernel,
        grid_spec=pltpu.PrefetchScalarGridSpec(
            num_scalar_prefetch=3,
            grid=(steps,),
            in_specs=[
                spec((heads, BQ, width), lambda i, *_: (0, i, 0)),
                whole(kx.shape),
                whole(kt.shape),
                whole(vs.shape),
                spec((BQ, heads * HEAD_DIM), lambda i, *_: (i, 0)),
                spec((heads, HEAD_DIM, BQ), lambda i, *_: (0, 0, i)),
                spec((heads, BQ), lambda i, *_: (0, i)),
            ],
            out_specs=whole((tokens, 3 * heads * HEAD_DIM)),
            scratch_shapes=[
                pltpu.VMEM((heads, tokens, HEAD_DIM), F32),
                pltpu.VMEM((heads, tokens, HEAD_DIM), F32),
                pltpu.VMEM((heads, HEAD_DIM, BQ), F32),
            ],
        ),
        out_shape=jax.ShapeDtypeStruct((tokens, 3 * heads * HEAD_DIM), BF),
        compiler_params=pltpu.CompilerParams(
            dimension_semantics=("arbitrary",), vmem_limit_bytes=52 << 20
        ),
        cost_estimate=pl.CostEstimate(
            flops=heads * tokens * tokens * HEAD_DIM * 10,
            bytes_accessed=heads * tokens * 2048,
            transcendentals=heads * tokens * tokens // 2,
        ),
        name="attend_back",
    )(count, listed, owned, qx, kx, kt, vs, up, out_wide, lse)


def head_split(matrix, parts):
    rows, cols = matrix.shape
    heads = cols // (parts * HEAD_DIM)
    each = heads // GROUP
    cube = matrix.reshape(rows, parts, heads, HEAD_DIM)
    own = cube[:, :, : each * GROUP].reshape(rows, parts, GROUP, each, HEAD_DIM)
    rest = jnp.broadcast_to(
        cube[:, :, None, each * GROUP :], (rows, parts, GROUP, heads - each * GROUP, HEAD_DIM)
    )
    joined = jnp.concatenate([own, rest], axis=3)
    return jnp.transpose(joined, (2, 0, 1, 3, 4)).reshape(GROUP, rows, -1)


def head_join(shares, parts, heads):
    group, rows, _ = shares.shape
    each = heads // GROUP
    cube = shares.astype(F32).reshape(group, rows, parts, -1, HEAD_DIM)
    own = jnp.transpose(cube[:, :, :, :each], (1, 2, 0, 3, 4)).reshape(
        rows, parts, each * GROUP, HEAD_DIM
    )
    rest = jnp.sum(cube[:, :, :, each:], axis=0)
    return jnp.concatenate([own, rest], axis=2).reshape(rows, -1)


def hidden_split(matrix, unit):
    rows = matrix.shape[0]
    cube = matrix.reshape(rows, -1, GROUP, unit)
    return jnp.transpose(cube, (2, 0, 1, 3)).reshape(GROUP, rows, -1)


def hidden_join(shares, unit):
    group, rows, _ = shares.shape
    cube = shares.reshape(group, rows, -1, unit)
    return jnp.transpose(cube, (1, 2, 0, 3)).reshape(rows, -1)


def exchange(shares):
    return lax.all_to_all(shares, PLANE, split_axis=0, concat_axis=0, tiled=True)


def take(stack, place):
    return lax.dynamic_index_in_dim(stack, place, 0, keepdims=False)


def columns_in(shard, width, split, place):
    if shard.size % width == 0:
        mine = exchange(split(shard.reshape(-1, width)))
        rows = mine.reshape(-1, mine.shape[-1])
        return lax.all_gather(rows, TREE, axis=0, tiled=True)
    full = lax.all_gather(shard, EVERY, axis=0, tiled=True).reshape(-1, width)
    return take(split(full), place)


def columns_out(grad, join, shard_shape, width, place):
    size = shard_shape[0] * shard_shape[1]
    if size % width == 0:
        rows = lax.psum_scatter(grad.astype(BF), TREE, scatter_dimension=0, tiled=True)
        shares = exchange(rows.reshape(GROUP, -1, rows.shape[-1]))
        return join(shares).astype(F32).reshape(shard_shape)
    spots = jnp.arange(GROUP, dtype=jnp.int32)[:, None, None] == place
    shares = jnp.where(spots, grad.astype(BF)[None], jnp.zeros((), BF))
    full = join(shares).astype(BF).reshape(-1, shard_shape[1])
    return lax.psum_scatter(full, EVERY, scatter_dimension=0, tiled=True).astype(F32)


def on_device(
    tokens,
    cotangent,
    w_qkv,
    w_out,
    w_fc,
    w_proj,
    ln1_gain,
    ln1_bias,
    q_bias,
    v_bias,
    out_bias,
    ln2_gain,
    ln2_bias,
    fc_bias,
    proj_bias,
    seg_lengths,
    parents,
):
    tok_dev, model_width = tokens.shape
    hidden = fc_bias.shape[0]
    flat_cols = w_qkv.shape[1]
    heads = model_width // HEAD_DIM
    each = heads // GROUP
    rest = heads - each * GROUP
    local = each + rest
    tree = lax.axis_index(TREE)
    place = (lax.axis_index("a") * 2 + lax.axis_index("b")) * 2 + lax.axis_index("c")
    device = tree * GROUP + place
    unit = max(1, hidden // lax.axis_size(EVERY))

    starts, ends, reach = tree_tables(take(seg_lengths, tree), take(parents, tree))
    position = jnp.arange(TREE_TOK, dtype=jnp.int32)
    hot = (
        (position[:, None] >= starts[None, :]) & (position[:, None] < ends[None, :])
    ).astype(F32)
    path = jnp.dot(hot, reach, preferred_element_type=F32)
    q_blocks, k_blocks = TREE_TOK // BQ, TREE_TOK // BK
    count, listed = block_lists(hot, path, q_blocks, k_blocks)
    block_numbers = jnp.arange(q_blocks, dtype=jnp.int32)
    turn = q_blocks - 1 - block_numbers
    owner = jnp.where(turn < GROUP, turn, 2 * GROUP - 2 - turn)
    owned = (owner == place).astype(jnp.int32)
    pad = LANES - HEAD_DIM - hot.shape[1]
    key_mark = jnp.pad(hot, ((0, 0), (0, pad))).astype(BF)
    query_mark = jnp.pad((1.0 - path) * NEGATIVE, ((0, 0), (0, pad))).astype(BF)

    w_qkv_l = columns_in(w_qkv, 3 * model_width, partial(head_split, parts=3), place)
    w_out_full = lax.all_gather(w_out, EVERY, axis=0, tiled=True).reshape(model_width, model_width)
    w_out_l = jnp.concatenate(
        [block_of(w_out_full, place, each * HEAD_DIM), w_out_full[each * GROUP * HEAD_DIM :]], axis=0
    )
    w_fc_l = columns_in(w_fc, hidden, partial(hidden_split, unit=unit), place)
    proj_whole = w_proj.size % model_width == 0
    if proj_whole:
        w_proj_l = lax.all_gather(w_proj.reshape(-1, model_width), TREE, axis=0, tiled=True)
    fc_bias_l = take(hidden_split(fc_bias[None], unit), place)[0]
    qkv_bias = jnp.concatenate([q_bias, jnp.zeros_like(q_bias), v_bias])
    qkv_bias_l = take(head_split(qkv_bias[None], 3), place)[0]

    residual_in = tokens.astype(F32)
    first_norm, normed_one, inv_one = norm_forward(residual_in, ln1_gain, ln1_bias)
    first_low = jnp.concatenate(plane_gather(first_norm.astype(BF)), axis=0)
    projected = (jnp.dot(first_low, w_qkv_l, preferred_element_type=F32) + qkv_bias_l).astype(BF)
    projected = xor_order(projected, place, tok_dev)
    cube = projected.reshape(TREE_TOK, 3, local, HEAD_DIM)
    score_scale = jnp.asarray(HEAD_DIM ** (-0.5), BF)
    marks = lambda mark: jnp.broadcast_to(mark[None], (local,) + mark.shape)
    qx = jnp.concatenate(
        [jnp.transpose(cube[:, 0], (1, 0, 2)) * score_scale, marks(query_mark)], axis=2
    )
    kx = jnp.concatenate([jnp.transpose(cube[:, 1], (1, 0, 2)), marks(key_mark)], axis=2)
    kt = jnp.transpose(cube[:, 1], (1, 2, 0))
    vs = jnp.transpose(cube[:, 2], (1, 0, 2))
    vt = jnp.transpose(cube[:, 2], (1, 2, 0))

    attended, out_wide, lse, tops = attend(count, listed, owned, qx, kx, vt)
    top_heads = jnp.max(tops, axis=1)
    spread = jnp.full((GROUP, each), NEGATIVE, F32)
    spread = lax.dynamic_update_slice(spread, top_heads[None, :each], (place, 0))
    logit_max = lax.pmax(jnp.concatenate([spread.reshape(-1), top_heads[each:]]), EVERY)

    attended = xor_order(attended, place, tok_dev)
    branch = jnp.dot(attended, w_out_l, preferred_element_type=F32).astype(BF)
    rows_of = lambda array: lambda r: array[r * tok_dev : (r + 1) * tok_dev]
    middle = residual_in + plane_scatter(rows_of(branch)) + out_bias

    second_norm, normed_two, inv_two = norm_forward(middle, ln2_gain, ln2_bias)
    second_low = jnp.concatenate(plane_gather(second_norm.astype(BF)), axis=0)
    grad_two = jnp.concatenate(plane_gather(cotangent), axis=0)
    if not proj_whole:
        proj_full = lax.all_gather(w_proj, EVERY, axis=0, tiled=True).reshape(hidden, model_width)
        w_proj_l = take(
            jnp.transpose(proj_full.reshape(-1, GROUP, unit, model_width), (1, 0, 2, 3)), place
        ).reshape(-1, model_width)
    pre_act = jnp.dot(second_low, w_fc_l, preferred_element_type=F32) + fc_bias_l
    activated, gelu_pull = jax.vjp(partial(jax.nn.gelu, approximate=True), pre_act)
    act_low = activated.astype(BF)
    branch_two = jnp.dot(act_low, w_proj_l, preferred_element_type=F32).astype(BF)
    output = (middle + plane_scatter(rows_of(branch_two)) + proj_bias).astype(BF)

    act_back = lax.dot_general(
        grad_two, w_proj_l, (((1,), (1,)), ((), ())), preferred_element_type=F32
    )
    pre_low = gelu_pull(act_back)[0].astype(BF)
    norm_back = lax.dot_general(
        pre_low, w_fc_l, (((1,), (1,)), ((), ())), preferred_element_type=F32
    ).astype(BF)
    over_rows = lambda left, right: lax.dot_general(
        left, right, (((0,), (0,)), ((), ())), preferred_element_type=F32
    )
    proj_grad = over_rows(act_low, grad_two)
    fc_grad = over_rows(second_low, pre_low)
    fc_bias_part = jnp.sum(pre_low.astype(F32), axis=0)

    grad_out = cotangent.astype(F32)
    proj_bias_grad = jnp.sum(grad_out, axis=0)
    mid_part, ln2_gain_grad, ln2_bias_grad = norm_backward(
        plane_scatter(rows_of(norm_back)), normed_two, inv_two, ln2_gain
    )
    middle_grad = grad_out + mid_part
    branch_own = middle_grad.astype(BF)
    out_bias_grad = jnp.sum(branch_own.astype(F32), axis=0)
    branch_low = jnp.concatenate(plane_gather(branch_own), axis=0)
    attn_back = lax.dot_general(
        branch_low, w_out_l, (((1,), (1,)), ((), ())), preferred_element_type=F32
    ).astype(BF)
    out_grad = over_rows(attended, branch_low)

    qkv_low = attend_back(
        count, listed, owned, qx, kx, kt, vs, xor_order(attn_back, place, tok_dev), out_wide, lse
    )
    qkv_low = xor_order(qkv_low, place, tok_dev)
    first_back = lax.dot_general(
        qkv_low, w_qkv_l, (((1,), (1,)), ((), ())), preferred_element_type=F32
    ).astype(BF)
    qkv_grad = over_rows(first_low, qkv_low)
    in_part, ln1_gain_grad, ln1_bias_grad = norm_backward(
        plane_scatter(rows_of(first_back)), normed_one, inv_one, ln1_gain
    )
    input_grad = middle_grad + in_part

    qkv_shard = columns_out(
        qkv_grad, partial(head_join, parts=3, heads=heads), w_qkv.shape, 3 * model_width, place
    )
    fc_shard = columns_out(fc_grad, partial(hidden_join, unit=unit), w_fc.shape, hidden, place)
    out_zero = jnp.zeros((each * GROUP * HEAD_DIM, model_width), BF)
    out_low = out_grad.astype(BF)
    out_rows = jnp.concatenate(
        [
            lax.dynamic_update_slice(
                out_zero, out_low[: each * HEAD_DIM], (place * each * HEAD_DIM, 0)
            ),
            out_low[each * HEAD_DIM :],
        ],
        axis=0,
    )
    out_shard = lax.psum_scatter(
        out_rows.reshape(-1, flat_cols), EVERY, scatter_dimension=0, tiled=True
    ).astype(F32)
    if proj_whole:
        proj_shard = (
            lax.psum_scatter(proj_grad.astype(BF), TREE, scatter_dimension=0, tiled=True)
            .astype(F32)
            .reshape(w_proj.shape)
        )
    else:
        spots = jnp.arange(GROUP, dtype=jnp.int32)[None, :, None, None] == place
        proj_rows = jnp.where(
            spots, proj_grad.astype(BF).reshape(-1, 1, unit, model_width), jnp.zeros((), BF)
        ).reshape(-1, flat_cols)
        proj_shard = lax.psum_scatter(proj_rows, EVERY, scatter_dimension=0, tiled=True).astype(F32)

    column_sums = jnp.sum(qkv_low.astype(F32), axis=0).reshape(3, local, HEAD_DIM)
    bias_parts = jnp.zeros((3, GROUP, each, HEAD_DIM), F32)
    bias_parts = lax.dynamic_update_slice(
        bias_parts, column_sums[:, None, :each], (0, place, 0, 0)
    )
    bias_parts = jnp.concatenate(
        [bias_parts.reshape(3, each * GROUP, HEAD_DIM), column_sums[:, each:]], axis=1
    ).reshape(3, model_width)
    fc_parts = jnp.zeros((GROUP, hidden // GROUP), F32)
    fc_parts = lax.dynamic_update_slice(fc_parts, fc_bias_part[None], (place, 0))
    fc_parts = hidden_join(fc_parts[:, None], unit)[0]
    small = lax.psum(
        (
            ln1_gain_grad,
            ln1_bias_grad,
            bias_parts[0],
            bias_parts[2],
            out_bias_grad,
            ln2_gain_grad,
            ln2_bias_grad,
            fc_parts,
            proj_bias_grad,
        ),
        EVERY,
    )

    clip_gain = jnp.sqrt(TAU / jnp.maximum(logit_max, TAU))
    rows_dev = w_qkv.shape[0]
    flat_index = (device * rows_dev + jnp.arange(rows_dev, dtype=jnp.int32)[:, None]) * flat_cols
    flat_index = flat_index + jnp.arange(flat_cols, dtype=jnp.int32)[None, :]
    column = flat_index % (3 * model_width)
    head_of = column % model_width // HEAD_DIM
    head_numbers = jnp.arange(heads, dtype=jnp.int32)
    head_gain = jnp.sum(
        jnp.where(
            head_of[:, :, None] == head_numbers[None, None, :], clip_gain[None, None, :], 0.0
        ),
        axis=2,
    )
    factor = jnp.where(column < 2 * model_width, head_gain, 1.0)
    clipped = (w_qkv.astype(F32) * factor).astype(BF)
    return (
        output,
        input_grad,
        qkv_shard,
        out_shard,
        fc_shard,
        proj_shard,
        *small,
        logit_max,
        clipped,
    )


def solution(mesh):
    split = Mesh(mesh.devices.reshape(-1, 2, 2, 2), EVERY)
    rows = P(EVERY, None)
    return jax.shard_map(
        on_device,
        mesh=split,
        in_specs=(rows,) * 6 + (P(),) * 11,
        out_specs=(rows,) * 6 + (P(),) * 10 + (rows,),
        check_vma=False,
    )
```

```python
from functools import partial

import jax
import jax.numpy as jnp
from jax import lax
from jax.experimental import pallas as pl
from jax.experimental.layout import Layout, with_layout_constraint
from jax.experimental.pallas import tpu as pltpu
from jax.sharding import Mesh, PartitionSpec as P

HEAD_DIM = 64
TREE_TOK = 2560
GROUP = 8

EPS = 1e-05
TAU = 7.0
NEGATIVE = -1e30

BQ = 256
BK = 256
LANES = 128

TREE = "t"
PLANE = ("a", "b", "c")
EVERY = ("t", "a", "b", "c")
BF = jnp.bfloat16
F32 = jnp.float32


def norm_forward(values, norm_gain, norm_shift):
    row_mean = jnp.mean(values, axis=-1, keepdims=True)
    centered = values - row_mean
    inv_std = lax.rsqrt(jnp.mean(centered * centered, axis=-1, keepdims=True) + EPS)
    normed = centered * inv_std
    return (normed * norm_gain + norm_shift, normed, inv_std)


def norm_backward(upstream, normed, inv_std, norm_gain):
    scaled = upstream * norm_gain
    inner = (
        scaled
        - jnp.mean(scaled, axis=-1, keepdims=True)
        - normed * jnp.mean(scaled * normed, axis=-1, keepdims=True)
    )
    return (inner * inv_std, jnp.sum(upstream * normed, axis=0), jnp.sum(upstream, axis=0))


def swap(value, axis):
    return lax.ppermute(value, axis, [(0, 1), (1, 0)])


def after(value, *others):
    return lax.optimization_barrier((value, *others))[0] if others else value


def rows_major(array):
    return with_layout_constraint(array, Layout(major_to_minor=tuple(range(array.ndim))))


def plane_write(blocks, other, place, base):
    rows = blocks[0].shape[0]
    full = base
    if full is None:
        full = jnp.zeros((GROUP * rows,) + blocks[0].shape[1:], blocks[0].dtype)
    for r, block in enumerate(blocks):
        for q, piece in ((2 * r, block), (2 * r + 1, other[r])):
            full = lax.dynamic_update_slice_in_dim(full, piece, (place ^ q) * rows, 0)
    return rows_major(full)


def plane_gather(own, place, base=None):
    half = own.shape[0] // 2
    from_b, from_a = swap(own, "b"), swap(own, "a")
    diag = jnp.concatenate([swap(from_b[:half], "a"), swap(from_a[half:], "b")], axis=0)
    blocks = (own, from_b, from_a, diag)
    full = plane_write(blocks, [swap(block, "c") for block in blocks], place, base)
    return full, (from_b, from_a)


def plane_fetch(own):
    across = lax.ppermute(own, ("a", "b"), [(i, i ^ 3) for i in range(4)])
    return (swap(own, "b"), swap(own, "a"), across)


def plane_scatter(array, place, hold=lambda sent: ()):
    rows = array.shape[0] // GROUP
    array = rows_major(array)
    sent = [block_of(array, place ^ r, rows) for r in range(GROUP)]
    sent = list(lax.optimization_barrier(tuple(sent)))
    came = tuple(swap(sent[r + 1], "c") for r in (6, 2, 4, 0))
    came = after(came, *hold(sent))
    diag, for_b, for_a, mine = (
        sent[r].astype(F32) + block.astype(F32) for r, block in zip((6, 2, 4, 0), came)
    )
    half = diag.shape[0] // 2
    top, bottom = lax.optimization_barrier((diag[:half].astype(BF), diag[half:].astype(BF)))
    top, bottom = swap(top, "b"), swap(bottom, "a")
    for_a = jnp.concatenate([for_a[:half] + top.astype(F32), for_a[half:]], axis=0).astype(BF)
    for_b = jnp.concatenate([for_b[:half], for_b[half:] + bottom.astype(F32)], axis=0).astype(BF)
    for_a, for_b = lax.optimization_barrier((for_a, for_b))
    total = mine + swap(for_b, "b").astype(F32) + swap(for_a, "a").astype(F32)
    return total, (for_a, for_b)


def block_of(array, index, rows):
    return lax.dynamic_slice_in_dim(array, index * rows, rows, 0)


def tree_parts(grad):
    count, me = lax.axis_size(TREE), lax.axis_index(TREE)
    rows = grad.shape[0] // count
    parts = [block_of(grad, me, rows)]
    for hop in range(1, count):
        sent = block_of(grad, (me + hop) % count, rows)
        pairs = [(i, (i + hop) % count) for i in range(count)]
        parts.append(lax.ppermute(sent, TREE, pairs))
    return tuple(parts)


def pairwise(values, combines, axis, pairs):
    others = [lax.ppermute(value, axis, pairs) for value in values]
    return [combine(*both) for combine, *both in zip(combines, values, others)]


def over_plane(values, combines):
    for axis in ("c", "b", "a"):
        values = pairwise(values, combines, axis, [(0, 1), (1, 0)])
    return values


def over_trees(values, combines):
    count = lax.axis_size(TREE)
    hop = 1
    while hop < count:
        values = pairwise(values, combines, TREE, [(i, i ^ hop) for i in range(count)])
        hop *= 2
    return values


def tree_tables(lengths, parent_row):
    count = lengths.shape[0]
    numbers = jnp.arange(count, dtype=jnp.int32)
    ends = jnp.sum(jnp.where(numbers[None, :] <= numbers[:, None], lengths[None, :], 0), axis=1)
    starts = ends - lengths
    reach = (
        (numbers[:, None] == numbers[None, :]) | (parent_row[:, None] == numbers[None, :])
    ).astype(F32)
    hops = 1
    while hops < count:
        reach = (
            jnp.sum(reach[:, :, None] * reach[None, :, :], axis=1) > 0.5
        ).astype(F32)
        hops *= 2
    return starts, ends, reach


def block_lists(hot, path, q_blocks, k_blocks):
    q_has = jnp.max(path.reshape(q_blocks, -1, path.shape[1]), axis=1)
    k_has = jnp.max(hot.reshape(k_blocks, -1, hot.shape[1]), axis=1)
    live = jnp.sum(q_has[:, None, :] * k_has[None, :, :], axis=2) > 0.5
    q_first = jnp.arange(q_blocks, dtype=jnp.int32) * (BQ // BK)
    keys = jnp.arange(k_blocks, dtype=jnp.int32)
    live = (live & (keys[None, :] < q_first[:, None])).astype(jnp.int32)
    rank = jnp.sum(
        jnp.where(keys[None, :, None] > keys[None, None, :], live[:, None, :], 0), axis=2
    )
    listed = jnp.sum(
        jnp.where(
            (rank[:, :, None] == keys[None, None, :]) & (live[:, :, None] > 0),
            keys[None, :, None],
            0,
        ),
        axis=1,
    )
    return jnp.sum(live, axis=1).astype(jnp.int32), listed.astype(jnp.int32)


def score_block(kx, qx):
    return lax.dot_general(kx, qx, (((1,), (1,)), ((), ())), preferred_element_type=F32)


def causal(key_first, query_first):
    keys = key_first + lax.broadcasted_iota(jnp.int32, (BK, BQ), 0)
    queries = query_first + lax.broadcasted_iota(jnp.int32, (BK, BQ), 1)
    return keys <= queries


def in_blocks(count, listed, step, group, some):
    others = count[step]

    @pl.when(others % 2 == 0)
    def _():
        for h in group:
            some(h, (step,), True)

    @pl.when(others % 2 == 1)
    def _():
        for h in group:
            some(h, (step, listed[step, others - 1]), True)

    def body(i, carry):
        for h in group:
            some(h, (listed[step, 2 * i], listed[step, 2 * i + 1]), False)
        return carry

    lax.fori_loop(0, others // 2, body, 0)


def head_cols(part, h, local):
    at = (part * local + h) * HEAD_DIM
    return slice(at, at + HEAD_DIM)


def attend_kernel(
    count, listed, owned, proj, q_mark, k_mark, out, out_wide, lse, top, kx, vt, qx, m_s, l_s, acc_s
):
    step = pl.program_id(0)
    q_first = step * BQ
    local = acc_s.shape[0]
    here = pl.ds(pl.multiple_of(q_first, BQ), BQ)

    @pl.when(step == 0)
    def _():
        top[...] = jnp.full(top.shape, NEGATIVE, F32)

    for h in range(local):
        kx[h, here, :] = jnp.concatenate([proj[:, head_cols(1, h, local)], k_mark[...]], axis=1)
        query = proj[:, head_cols(0, h, local)] * jnp.asarray(HEAD_DIM ** (-0.5), BF)
        qx[h] = jnp.concatenate([query, q_mark[...]], axis=1)
    vt[:, here] = proj[:, 2 * local * HEAD_DIM :].T

    def some(h, blocks, diagonal):
        rows = [pl.ds(pl.multiple_of(kb * BK, BK), BK) for kb in blocks]
        scores = [score_block(kx[h, r, :], qx[h]) for r in rows]
        if diagonal:
            scores[0] = jnp.where(causal(blocks[0] * BK, q_first), scores[0], NEGATIVE)
        old = m_s[h : h + 1, :]
        new = old
        for score in scores:
            new = jnp.maximum(new, jnp.max(score, axis=0, keepdims=True))
        weights = [jnp.exp(score - new) for score in scores]
        shrink = jnp.exp(old - new)
        m_s[h : h + 1, :] = new
        l_s[h : h + 1, :] = l_s[h : h + 1, :] * shrink + sum(
            jnp.sum(weight, axis=0, keepdims=True) for weight in weights
        )
        acc_s[h] = acc_s[h] * shrink + sum(
            jnp.dot(
                vt[h * HEAD_DIM : (h + 1) * HEAD_DIM, r],
                weight.astype(BF),
                preferred_element_type=F32,
            )
            for r, weight in zip(rows, weights)
        )

    def heads(group):
        for h in group:
            m_s[h : h + 1, :] = jnp.full((1, BQ), NEGATIVE, F32)
            l_s[h : h + 1, :] = jnp.zeros((1, BQ), F32)
            acc_s[h] = jnp.zeros((HEAD_DIM, BQ), F32)
        in_blocks(count, listed, step, group, some)
        for h in group:
            total = l_s[h : h + 1, :]
            out_wide[h] = acc_s[h] / total
            lse[h : h + 1, :] = m_s[h : h + 1, :] + jnp.log(total)
            top[h : h + 1, :] = jnp.maximum(top[h : h + 1, :], m_s[h : h + 1, :])

    last = local - 1
    heads(range(last))

    @pl.when(owned[step] > 0)
    def _():
        heads([last])

    @pl.when(owned[step] == 0)
    def _():
        out_wide[last] = jnp.zeros((HEAD_DIM, BQ), F32)
        lse[last : last + 1, :] = jnp.zeros((1, BQ), F32)

    for h in range(local):
        out[:, h * HEAD_DIM : (h + 1) * HEAD_DIM] = out_wide[h].T.astype(BF)


def whole_block(shape):
    return pl.BlockSpec(shape, lambda i, *_: (0,) * len(shape), pipeline_mode=pl.Buffered(1))


def attend(count, listed, owned, proj, q_mark, k_mark):
    tokens, width = proj.shape
    heads = width // (3 * HEAD_DIM)
    return pl.pallas_call(
        attend_kernel,
        grid_spec=pltpu.PrefetchScalarGridSpec(
            num_scalar_prefetch=3,
            grid=(tokens // BQ,),
            in_specs=[
                pl.BlockSpec((BQ, width), lambda i, *_: (i, 0)),
                pl.BlockSpec((BQ, q_mark.shape[1]), lambda i, *_: (i, 0)),
                pl.BlockSpec((BQ, k_mark.shape[1]), lambda i, *_: (i, 0)),
            ],
            out_specs=[
                pl.BlockSpec((BQ, heads * HEAD_DIM), lambda i, *_: (i, 0)),
                pl.BlockSpec((heads, HEAD_DIM, BQ), lambda i, *_: (0, 0, i)),
                pl.BlockSpec((heads, BQ), lambda i, *_: (0, i)),
                pl.BlockSpec((heads, BQ), lambda i, *_: (0, 0)),
            ],
            scratch_shapes=[
                pltpu.VMEM((heads, tokens, LANES), BF),
                pltpu.VMEM((heads * HEAD_DIM, tokens), BF),
                pltpu.VMEM((heads, BQ, LANES), BF),
                pltpu.VMEM((heads, BQ), F32),
                pltpu.VMEM((heads, BQ), F32),
                pltpu.VMEM((heads, HEAD_DIM, BQ), F32),
            ],
        ),
        out_shape=[
            jax.ShapeDtypeStruct((tokens, heads * HEAD_DIM), BF),
            jax.ShapeDtypeStruct((heads, HEAD_DIM, tokens), F32),
            jax.ShapeDtypeStruct((heads, tokens), F32),
            jax.ShapeDtypeStruct((heads, BQ), F32),
        ],
        compiler_params=pltpu.CompilerParams(
            dimension_semantics=("arbitrary",), vmem_limit_bytes=32 << 20
        ),
        cost_estimate=pl.CostEstimate(
            flops=heads * tokens * tokens * HEAD_DIM * 4,
            bytes_accessed=heads * tokens * 1024,
            transcendentals=heads * tokens * tokens // 2,
        ),
        name="attend",
    )(count, listed, owned, proj, q_mark, k_mark)


def attend_back_kernel(
    count, listed, owned, proj, q_mark, k_mark, up, out_wide, lse, grads, kx, kt, vs, qx, dk_s, dv_s, dq_s
):
    step = pl.program_id(0)
    q_first = step * BQ
    local = dq_s.shape[0]
    last = local - 1
    width = local * HEAD_DIM
    here = pl.ds(pl.multiple_of(q_first, BQ), BQ)

    for h in range(local):
        kx[h, here, :] = jnp.concatenate([proj[:, head_cols(1, h, local)], k_mark[...]], axis=1)
        query = proj[:, head_cols(0, h, local)] * jnp.asarray(HEAD_DIM ** (-0.5), BF)
        qx[h] = jnp.concatenate([query, q_mark[...]], axis=1)
        vs[h, here, :] = proj[:, head_cols(2, h, local)]
        dk_s[h, here, :] = jnp.zeros((BQ, HEAD_DIM), F32)
        dv_s[h, here, :] = jnp.zeros((BQ, HEAD_DIM), F32)
    kt[:, here] = proj[:, width : 2 * width].T

    def heads(group):
        parts = {}
        for h in group:
            rows_up = up[:, h * HEAD_DIM : (h + 1) * HEAD_DIM]
            cols_up = rows_up.astype(F32).T
            delta = jnp.sum(out_wide[h] * cols_up, axis=0, keepdims=True)
            parts[h] = (rows_up, cols_up.astype(BF), delta, lse[h : h + 1, :])
            dq_s[h] = jnp.zeros((HEAD_DIM, BQ), F32)

        def some(h, blocks, diagonal):
            rows_up, cols_up, delta, norm = parts[h]
            rows = [pl.ds(pl.multiple_of(kb * BK, BK), BK) for kb in blocks]
            probs = [jnp.exp(score_block(kx[h, r, :], qx[h]) - norm) for r in rows]
            if diagonal:
                probs[0] = jnp.where(causal(blocks[0] * BK, q_first), probs[0], 0.0)
            dprobs = [jnp.dot(vs[h, r, :], cols_up, preferred_element_type=F32) for r in rows]
            dscores = [(p * (d - delta)).astype(BF) for p, d in zip(probs, dprobs)]
            for r, p, d in zip(rows, probs, dscores):
                dv_s[h, r, :] += jnp.dot(p.astype(BF), rows_up, preferred_element_type=F32)
                dk_s[h, r, :] += jnp.dot(d, qx[h][:, :HEAD_DIM], preferred_element_type=F32)
            dq_s[h] += sum(
                jnp.dot(
                    kt[h * HEAD_DIM : (h + 1) * HEAD_DIM, r], d, preferred_element_type=F32
                )
                for r, d in zip(rows, dscores)
            )

        in_blocks(count, listed, step, group, some)

    heads(range(last))

    @pl.when(owned[step] > 0)
    def _():
        heads([last])

    @pl.when(owned[step] == 0)
    def _():
        dq_s[last] = jnp.zeros((HEAD_DIM, BQ), F32)

    for h in range(local):
        grads[here, h * HEAD_DIM : (h + 1) * HEAD_DIM] = (
            dq_s[h] * (HEAD_DIM ** (-0.5))
        ).T.astype(BF)

    @pl.when(step == pl.num_programs(0) - 1)
    def _():
        for h in range(local):
            at = width + h * HEAD_DIM
            grads[:, at : at + HEAD_DIM] = dk_s[h].astype(BF)
            at = 2 * width + h * HEAD_DIM
            grads[:, at : at + HEAD_DIM] = dv_s[h].astype(BF)


def attend_back(count, listed, owned, proj, q_mark, k_mark, up, out_wide, lse):
    tokens, width = proj.shape
    heads = width // (3 * HEAD_DIM)
    return pl.pallas_call(
        attend_back_kernel,
        grid_spec=pltpu.PrefetchScalarGridSpec(
            num_scalar_prefetch=3,
            grid=(tokens // BQ,),
            in_specs=[
                pl.BlockSpec((BQ, width), lambda i, *_: (i, 0)),
                pl.BlockSpec((BQ, q_mark.shape[1]), lambda i, *_: (i, 0)),
                pl.BlockSpec((BQ, k_mark.shape[1]), lambda i, *_: (i, 0)),
                pl.BlockSpec((BQ, heads * HEAD_DIM), lambda i, *_: (i, 0)),
                pl.BlockSpec((heads, HEAD_DIM, BQ), lambda i, *_: (0, 0, i)),
                pl.BlockSpec((heads, BQ), lambda i, *_: (0, i)),
            ],
            out_specs=whole_block((tokens, width)),
            scratch_shapes=[
                pltpu.VMEM((heads, tokens, LANES), BF),
                pltpu.VMEM((heads * HEAD_DIM, tokens), BF),
                pltpu.VMEM((heads, tokens, HEAD_DIM), BF),
                pltpu.VMEM((heads, BQ, LANES), BF),
                pltpu.VMEM((heads, tokens, HEAD_DIM), F32),
                pltpu.VMEM((heads, tokens, HEAD_DIM), F32),
                pltpu.VMEM((heads, HEAD_DIM, BQ), F32),
            ],
        ),
        out_shape=jax.ShapeDtypeStruct((tokens, width), BF),
        compiler_params=pltpu.CompilerParams(
            dimension_semantics=("arbitrary",), vmem_limit_bytes=44 << 20
        ),
        cost_estimate=pl.CostEstimate(
            flops=heads * tokens * tokens * HEAD_DIM * 10,
            bytes_accessed=heads * tokens * 2048,
            transcendentals=heads * tokens * tokens // 2,
        ),
        name="attend_back",
    )(count, listed, owned, proj, q_mark, k_mark, up, out_wide, lse)


def head_split(matrix, parts):
    rows, cols = matrix.shape
    heads = cols // (parts * HEAD_DIM)
    each = heads // GROUP
    cube = matrix.reshape(rows, parts, heads, HEAD_DIM)
    own = cube[:, :, : each * GROUP].reshape(rows, parts, GROUP, each, HEAD_DIM)
    rest = jnp.broadcast_to(
        cube[:, :, None, each * GROUP :], (rows, parts, GROUP, heads - each * GROUP, HEAD_DIM)
    )
    joined = jnp.concatenate([own, rest], axis=3)
    return jnp.transpose(joined, (2, 0, 1, 3, 4)).reshape(GROUP, rows, -1)


def head_join(shares, parts, heads):
    group, rows, _ = shares.shape
    each = heads // GROUP
    cube = shares.astype(F32).reshape(group, rows, parts, -1, HEAD_DIM)
    own = jnp.transpose(cube[:, :, :, :each], (1, 2, 0, 3, 4)).reshape(
        rows, parts, each * GROUP, HEAD_DIM
    )
    rest = jnp.sum(cube[:, :, :, each:], axis=0)
    return jnp.concatenate([own, rest], axis=2).reshape(rows, -1)


def hidden_split(matrix, unit):
    rows = matrix.shape[0]
    cube = matrix.reshape(rows, -1, GROUP, unit)
    return jnp.transpose(cube, (2, 0, 1, 3)).reshape(GROUP, rows, -1)


def hidden_join(shares, unit):
    group, rows, _ = shares.shape
    cube = shares.reshape(group, rows, -1, unit)
    return jnp.transpose(cube, (1, 2, 0, 3)).reshape(rows, -1)


def exchange(shares):
    return lax.all_to_all(shares, PLANE, split_axis=0, concat_axis=0, tiled=True)


def take(stack, place):
    return lax.dynamic_index_in_dim(stack, place, 0, keepdims=False)


def columns_start(shard, width, split):
    if shard.size % width == 0:
        mine = exchange(split(shard.reshape(-1, width)))
        return mine.reshape(-1, mine.shape[-1])
    return shard


def columns_end(rows, size, width, split, place):
    if size % width == 0:
        return lax.all_gather(rows, TREE, axis=0, tiled=True)
    full = lax.all_gather(rows, EVERY, axis=0, tiled=True).reshape(-1, width)
    return take(split(full), place)


def columns_first(grad, size, width):
    if size % width == 0:
        rows = lax.psum_scatter(grad, TREE, scatter_dimension=0, tiled=True)
        return rows.reshape(GROUP, -1, rows.shape[-1])
    return grad


def columns_second(slots, join, shard_shape, width, place):
    if shard_shape[0] * shard_shape[1] % width == 0:
        return join(slots).astype(F32).reshape(shard_shape)
    spots = jnp.arange(GROUP, dtype=jnp.int32)[:, None, None] == place
    shares = jnp.where(spots, slots[None], jnp.zeros((), BF))
    full = join(shares).astype(BF).reshape(-1, shard_shape[1])
    return lax.psum_scatter(full, EVERY, scatter_dimension=0, tiled=True).astype(F32)


def owner_rows(share, trees):
    t, p, i = (
        lax.broadcasted_iota(jnp.int32, (trees, GROUP, share), dim) for dim in range(3)
    )
    return (t * GROUP + p) * share + i


def slots_out(columns, own, share, place):
    rows = owner_rows(share, lax.axis_size(TREE)) - place * own
    numbers = jnp.arange(own, dtype=jnp.int32)
    pick = jnp.any(rows[..., None] == numbers, axis=0).reshape(-1, own).astype(BF)
    slots = lax.dot_general(
        pick, columns[:, :own], (((1,), (1,)), ((), ())), preferred_element_type=F32
    )
    return slots.astype(BF).reshape(GROUP, share, -1)


def slots_in(slots, own, share, place, padded):
    trees = lax.axis_size(TREE)
    rows = take(jnp.swapaxes(owner_rows(share, trees), 0, 1), place)
    total = jnp.zeros((trees,) + slots.shape[1:], slots.dtype)
    for source in range(GROUP):
        held = (rows >= source * own) & (rows < (source + 1) * own)
        total = jnp.where(held[:, :, None], slots[source][None], total)
    return jnp.pad(total, ((0, 0), (0, padded - share), (0, 0))).reshape(trees * padded, -1)


def on_device(
    tokens,
    cotangent,
    w_qkv,
    w_out,
    w_fc,
    w_proj,
    ln1_gain,
    ln1_bias,
    q_bias,
    v_bias,
    out_bias,
    ln2_gain,
    ln2_bias,
    fc_bias,
    proj_bias,
    seg_lengths,
    parents,
):
    tok_dev, model_width = tokens.shape
    hidden = fc_bias.shape[0]
    flat_cols = w_qkv.shape[1]
    heads = model_width // HEAD_DIM
    each = heads // GROUP
    rest = heads - each * GROUP
    local = each + rest
    tree = lax.axis_index(TREE)
    place = (lax.axis_index("a") * 2 + lax.axis_index("b")) * 2 + lax.axis_index("c")
    device = tree * GROUP + place
    unit = max(1, hidden // lax.axis_size(EVERY))

    starts, ends, reach = tree_tables(take(seg_lengths, tree), take(parents, tree))
    position = jnp.arange(TREE_TOK, dtype=jnp.int32)
    hot = (
        (position[:, None] >= starts[None, :]) & (position[:, None] < ends[None, :])
    ).astype(F32)
    path = jnp.dot(hot, reach, preferred_element_type=F32)
    q_blocks, k_blocks = TREE_TOK // BQ, TREE_TOK // BK
    count, listed = block_lists(hot, path, q_blocks, k_blocks)
    block_numbers = jnp.arange(q_blocks, dtype=jnp.int32)
    turn = q_blocks - 1 - block_numbers
    owner = jnp.where(turn < GROUP, turn, 2 * GROUP - 2 - turn)
    owned = (owner == place).astype(jnp.int32)
    pad = LANES - HEAD_DIM - hot.shape[1]
    k_mark = jnp.pad(hot, ((0, 0), (0, pad))).astype(BF)
    q_mark = jnp.pad((1.0 - path) * NEGATIVE, ((0, 0), (0, pad))).astype(BF)

    residual_in = tokens.astype(F32)
    first_norm, normed_one, inv_one = norm_forward(residual_in, ln1_gain, ln1_bias)
    first_own = first_norm.astype(BF)
    qkv_split, fc_split = partial(head_split, parts=3), partial(hidden_split, unit=unit)
    qkv_rows = columns_start(after(w_qkv, first_own), 3 * model_width, qkv_split)
    w_qkv_l = columns_end(qkv_rows, w_qkv.size, 3 * model_width, qkv_split, place)
    qkv_bias = jnp.concatenate([q_bias, jnp.zeros_like(q_bias), v_bias])
    qkv_bias_l = take(head_split(qkv_bias[None], 3), place)[0]
    first_low, _ = plane_gather(first_own, place)

    two_far = plane_fetch(after(cotangent, first_low))
    whole_rows = w_out.size % model_width == 0
    ratio = model_width // flat_cols
    w_out_full = lax.all_gather(after(w_out, first_low), EVERY, axis=0, tiled=True)
    w_out_l = jnp.concatenate(
        [
            block_of(w_out_full, place, each * HEAD_DIM * ratio),
            w_out_full[each * GROUP * HEAD_DIM * ratio :],
        ],
        axis=0,
    ).reshape(-1, model_width)
    proj_whole = w_proj.size % model_width == 0
    if proj_whole:
        w_proj_l = lax.all_gather(
            after(w_proj.reshape(-1, model_width), first_low), TREE, axis=0, tiled=True
        )
    else:
        proj_full = lax.all_gather(w_proj, EVERY, axis=0, tiled=True).reshape(hidden, model_width)
        w_proj_l = take(
            jnp.transpose(proj_full.reshape(-1, GROUP, unit, model_width), (1, 0, 2, 3)), place
        ).reshape(-1, model_width)
    fc_bias_l = take(hidden_split(fc_bias[None], unit), place)[0]
    projected = (jnp.dot(first_low, w_qkv_l, preferred_element_type=F32) + qkv_bias_l).astype(BF)

    fc_rows = columns_start(after(w_fc, projected), hidden, fc_split)
    attended, out_wide, lse, tops = attend(count, listed, owned, projected, q_mark, k_mark)
    attended, two_far, fc_rows = lax.optimization_barrier((attended, two_far, fc_rows))
    w_fc_l = columns_end(fc_rows, w_fc.size, hidden, fc_split, place)
    branch = jnp.dot(attended, w_out_l, preferred_element_type=F32).astype(BF)
    mid_sum, mid_last = plane_scatter(branch, place)
    two_blocks = after((cotangent,) + two_far, *mid_last)
    grad_two = plane_write(two_blocks, [swap(block, "c") for block in two_blocks], place, None)
    middle = residual_in + mid_sum + out_bias

    second_norm, normed_two, inv_two = norm_forward(middle, ln2_gain, ln2_bias)
    second_own = second_norm.astype(BF)
    second_low, _ = plane_gather(second_own, place, branch)
    own_slots = ()
    if whole_rows:
        share = w_out.size // model_width
        own_slots = slots_out(after(attended, second_own), each * HEAD_DIM, share, place)
        own_slots = exchange(after(own_slots, second_low))
    pre_act = jnp.dot(second_low, w_fc_l, preferred_element_type=F32) + fc_bias_l
    activated, gelu_pull = jax.vjp(partial(jax.nn.gelu, approximate=True), pre_act)
    act_low = activated.astype(BF)
    over_cols = lambda left, right: lax.dot_general(
        left, right, (((1,), (1,)), ((), ())), preferred_element_type=F32
    )
    over_rows = lambda left, right: lax.dot_general(
        left, right, (((0,), (0,)), ((), ())), preferred_element_type=F32
    )
    pre_low = gelu_pull(over_cols(grad_two, w_proj_l))[0].astype(BF)
    norm_back = over_cols(pre_low, w_fc_l).astype(BF)
    norm_back, own_slots = lax.optimization_barrier((norm_back, own_slots))
    back_sum, back_last = plane_scatter(norm_back, place)

    grad_out = cotangent.astype(F32)
    proj_bias_grad = jnp.sum(grad_out, axis=0)
    mid_part, ln2_gain_grad, ln2_bias_grad = norm_backward(back_sum, normed_two, inv_two, ln2_gain)
    middle_grad = grad_out + mid_part
    branch_own = middle_grad.astype(BF)
    out_bias_grad = jnp.sum(branch_own.astype(F32), axis=0)

    branch_low, _ = plane_gather(branch_own, place, norm_back)

    fc_low = over_rows(second_low, after(pre_low, branch_own)).astype(BF)
    proj_low = over_rows(after(act_low, branch_own), grad_two).astype(BF)
    branch_two = jnp.dot(
        after(act_low, proj_low), w_proj_l, preferred_element_type=F32
    ).astype(BF)
    attn_back = over_cols(branch_low, w_out_l).astype(BF)
    attn_back = after(attn_back, branch_two)

    two_sum = lax.psum_scatter(
        after(branch_two, branch_low), PLANE, scatter_dimension=0, tiled=True
    )
    fc_rows = columns_first(fc_low, w_fc.size, hidden)
    proj_parts = tree_parts(proj_low) if proj_whole else ()
    qkv_low = attend_back(
        count, listed, owned, projected, q_mark, k_mark, attn_back, out_wide, lse
    )
    qkv_low, fc_rows, proj_parts = lax.optimization_barrier((qkv_low, fc_rows, proj_parts))
    if w_fc.size % hidden == 0:
        fc_rows = exchange(fc_rows)
    first_back = over_cols(qkv_low, w_qkv_l).astype(BF)
    made = []

    def beside(sent):
        made.append(over_rows(first_low, after(qkv_low, two_sum, *sent)).astype(BF))
        return made + [fc_rows]

    in_sum, in_last = plane_scatter(first_back, place, beside)
    qkv_rows = columns_first(made[0], w_qkv.size, 3 * model_width)
    branch_late = after(branch_low, *in_last)
    if whole_rows:
        padded = -(-share // 16) * 16
        out_rows = jnp.dot(
            slots_in(own_slots, each * HEAD_DIM, share, place, padded),
            branch_late,
            preferred_element_type=F32,
        ).astype(BF)
        out_rows = lax.psum_scatter(
            after(out_rows, qkv_rows), TREE, scatter_dimension=0, tiled=True
        )
        common = over_rows(attended[:, each * HEAD_DIM :], branch_late).astype(BF)
    else:
        out_low = over_rows(attended, branch_late).astype(BF)
        common = jnp.zeros((8, LANES), BF)
    in_part, ln1_gain_grad, ln1_bias_grad = norm_backward(in_sum, normed_one, inv_one, ln1_gain)

    fc_bias_part = jnp.sum(after(pre_low, *in_last).astype(F32), axis=0)
    fc_parts = jnp.zeros((GROUP, hidden // GROUP), F32)
    fc_parts = lax.dynamic_update_slice(fc_parts, fc_bias_part[None], (place, 0))
    fc_parts = hidden_join(fc_parts[:, None], unit)[0]
    column_sums = jnp.sum(after(qkv_low, *in_last).astype(F32), axis=0)
    column_sums = column_sums.reshape(3, local, HEAD_DIM)
    bias_parts = jnp.zeros((3, GROUP, each, HEAD_DIM), F32)
    bias_parts = lax.dynamic_update_slice(
        bias_parts, column_sums[:, None, :each], (0, place, 0, 0)
    )
    bias_parts = jnp.concatenate(
        [bias_parts.reshape(3, each * GROUP, HEAD_DIM), column_sums[:, each:]], axis=1
    ).reshape(3, model_width)
    sums = jnp.concatenate(
        [
            ln1_gain_grad,
            ln1_bias_grad,
            bias_parts[0],
            bias_parts[2],
            out_bias_grad,
            ln2_gain_grad,
            ln2_bias_grad,
            proj_bias_grad,
            fc_parts,
        ]
    )
    top_heads = jnp.max(tops, axis=1)
    spread = jnp.full((GROUP, each), NEGATIVE, F32)
    spread = lax.dynamic_update_slice(spread, top_heads[None, :each], (place, 0))
    spread = jnp.concatenate([spread.reshape(-1), top_heads[each:]])
    is_sum = jnp.arange(sums.shape[0] + heads, dtype=jnp.int32) < sums.shape[0]
    combine = lambda left, right: jnp.where(is_sum, left + right, jnp.maximum(left, right))
    sums = jnp.concatenate([sums, spread])

    whole_qkv = w_qkv.size % (3 * model_width) == 0
    combines = [combine, lambda left, right: left + right]
    sums, common = over_plane(lax.optimization_barrier((sums, common)), combines)
    if whole_qkv:
        qkv_rows = exchange(after(qkv_rows, in_sum))
    sums, common, qkv_rows = lax.optimization_barrier((sums, common, qkv_rows))
    sums, common = over_trees([sums, common], combines)
    logit_max = sums[-heads:]
    qkv_shard = columns_second(
        qkv_rows, partial(head_join, parts=3, heads=heads), w_qkv.shape, 3 * model_width, place
    )
    fc_shard = columns_second(
        after(fc_rows, sums), partial(hidden_join, unit=unit), w_fc.shape, hidden, place
    )
    if whole_rows:
        rows = device * share + jnp.arange(share, dtype=jnp.int32) - GROUP * each * HEAD_DIM
        numbers = jnp.arange(common.shape[0], dtype=jnp.int32)
        pick = (rows[:, None] == numbers[None, :]).astype(BF)
        out_shard = out_rows[:share].astype(F32) + jnp.dot(
            pick, common, preferred_element_type=F32
        )
        out_shard = out_shard.reshape(w_out.shape)
    else:
        out_zero = jnp.zeros((each * GROUP * HEAD_DIM, model_width), BF)
        out_rows = jnp.concatenate(
            [
                lax.dynamic_update_slice(
                    out_zero, out_low[: each * HEAD_DIM], (place * each * HEAD_DIM, 0)
                ),
                out_low[each * HEAD_DIM :],
            ],
            axis=0,
        ).reshape(-1, flat_cols)
        out_shard = lax.psum_scatter(out_rows, EVERY, scatter_dimension=0, tiled=True).astype(F32)
    if proj_whole:
        proj_shard = sum(part.astype(F32) for part in after(proj_parts, in_sum))
        proj_shard = proj_shard.reshape(w_proj.shape)
    else:
        spots = jnp.arange(GROUP, dtype=jnp.int32)[None, :, None, None] == place
        proj_rows = jnp.where(
            spots, proj_low.reshape(-1, 1, unit, model_width), jnp.zeros((), BF)
        ).reshape(-1, flat_cols)
        proj_shard = lax.psum_scatter(proj_rows, EVERY, scatter_dimension=0, tiled=True).astype(F32)
    input_grad = middle_grad + in_part
    output = (middle + after(two_sum, sums).astype(F32) + proj_bias).astype(BF)

    cut = lambda array, i: array[i * model_width : (i + 1) * model_width]
    small = (
        *(cut(sums, i) for i in range(7)),
        sums[8 * model_width : -heads],
        cut(sums, 7),
    )

    clip_gain = jnp.sqrt(TAU / jnp.maximum(logit_max, TAU))
    rows_dev = w_qkv.shape[0]
    flat_index = (after(device, in_sum) * rows_dev + jnp.arange(rows_dev, dtype=jnp.int32)[:, None]) * flat_cols
    flat_index = flat_index + jnp.arange(flat_cols, dtype=jnp.int32)[None, :]
    column = flat_index % (3 * model_width)
    head_of = column % model_width // HEAD_DIM
    head_numbers = jnp.arange(heads, dtype=jnp.int32)
    head_gain = jnp.sum(
        jnp.where(
            head_of[:, :, None] == head_numbers[None, None, :], clip_gain[None, None, :], 0.0
        ),
        axis=2,
    )
    factor = jnp.where(column < 2 * model_width, head_gain, 1.0)
    clipped = (w_qkv.astype(F32) * factor).astype(BF)
    return (
        output,
        input_grad,
        qkv_shard,
        out_shard,
        fc_shard,
        proj_shard,
        *small,
        logit_max,
        clipped,
    )


def solution(mesh):
    split = Mesh(mesh.devices.reshape(-1, 2, 2, 2), EVERY)
    rows = P(EVERY, None)
    return jax.shard_map(
        on_device,
        mesh=split,
        in_specs=(rows,) * 6 + (P(),) * 11,
        out_specs=(rows,) * 6 + (P(),) * 10 + (rows,),
        check_vma=False,
    )
```

```python
from functools import partial

import jax
import jax.numpy as jnp
from jax import lax
from jax.experimental import pallas as pl
from jax.experimental.layout import Layout, with_layout_constraint
from jax.experimental.pallas import tpu as pltpu
from jax.sharding import Mesh, PartitionSpec as P

HEAD_DIM = 64
TREE_TOK = 2560
GROUP = 8

EPS = 1e-05
TAU = 7.0
NEGATIVE = -1e30

BQ = 256
BK = 256
LANES = 128

TREE = "t"
PLANE = ("a", "b", "c")
EVERY = ("t", "a", "b", "c")
BF = jnp.bfloat16
F32 = jnp.float32


def norm_forward(values, norm_gain, norm_shift):
    row_mean = jnp.mean(values, axis=-1, keepdims=True)
    centered = values - row_mean
    inv_std = lax.rsqrt(jnp.mean(centered * centered, axis=-1, keepdims=True) + EPS)
    normed = centered * inv_std
    return (normed * norm_gain + norm_shift, normed, inv_std)


def norm_backward(upstream, normed, inv_std, norm_gain):
    scaled = upstream * norm_gain
    inner = (
        scaled
        - jnp.mean(scaled, axis=-1, keepdims=True)
        - normed * jnp.mean(scaled * normed, axis=-1, keepdims=True)
    )
    return (inner * inv_std, jnp.sum(upstream * normed, axis=0), jnp.sum(upstream, axis=0))


def swap(value, axis):
    return lax.ppermute(value, axis, [(0, 1), (1, 0)])


def after(value, *others):
    return lax.optimization_barrier((value, *others))[0] if others else value


def rows_major(array):
    return with_layout_constraint(array, Layout(major_to_minor=tuple(range(array.ndim))))


def plane_write(blocks, other, place, base):
    rows = blocks[0].shape[0]
    full = base
    if full is None:
        full = jnp.zeros((GROUP * rows,) + blocks[0].shape[1:], blocks[0].dtype)
    for r, block in enumerate(blocks):
        for q, piece in ((2 * r, block), (2 * r + 1, other[r])):
            full = lax.dynamic_update_slice_in_dim(full, piece, (place ^ q) * rows, 0)
    return rows_major(full)


def plane_gather(own, place, base=None):
    half = own.shape[0] // 2
    from_b, from_a = swap(own, "b"), swap(own, "a")
    diag = jnp.concatenate([swap(from_b[:half], "a"), swap(from_a[half:], "b")], axis=0)
    blocks = (own, from_b, from_a, diag)
    full = plane_write(blocks, [swap(block, "c") for block in blocks], place, base)
    return full, (from_b, from_a)


def plane_near(own):
    return swap(own, "b"), swap(own, "a")


def plane_far(from_b, from_a):
    half = from_b.shape[0] // 2
    return jnp.concatenate([swap(from_b[:half], "a"), swap(from_a[half:], "b")], axis=0)


def plane_scatter(array, place, hold=lambda sent: ()):
    rows = array.shape[0] // GROUP
    array = rows_major(array)
    sent = [block_of(array, place ^ r, rows) for r in range(GROUP)]
    sent = list(lax.optimization_barrier(tuple(sent)))
    came = tuple(swap(sent[r + 1], "c") for r in (6, 2, 4, 0))
    came = after(came, *hold(sent))
    diag, for_b, for_a, mine = (
        sent[r].astype(F32) + block.astype(F32) for r, block in zip((6, 2, 4, 0), came)
    )
    half = diag.shape[0] // 2
    top, bottom = lax.optimization_barrier((diag[:half].astype(BF), diag[half:].astype(BF)))
    top, bottom = swap(top, "b"), swap(bottom, "a")
    for_a = jnp.concatenate([for_a[:half] + top.astype(F32), for_a[half:]], axis=0).astype(BF)
    for_b = jnp.concatenate([for_b[:half], for_b[half:] + bottom.astype(F32)], axis=0).astype(BF)
    for_a, for_b = lax.optimization_barrier((for_a, for_b))
    total = mine + swap(for_b, "b").astype(F32) + swap(for_a, "a").astype(F32)
    return total, (for_a, for_b)


def block_of(array, index, rows):
    return lax.dynamic_slice_in_dim(array, index * rows, rows, 0)


def tree_parts(grad):
    count, me = lax.axis_size(TREE), lax.axis_index(TREE)
    rows = grad.shape[0] // count
    parts = [block_of(grad, me, rows)]
    for hop in range(1, count):
        sent = block_of(grad, (me + hop) % count, rows)
        pairs = [(i, (i + hop) % count) for i in range(count)]
        parts.append(lax.ppermute(sent, TREE, pairs))
    return tuple(parts)


def pairwise(values, combines, axis, pairs):
    others = [lax.ppermute(value, axis, pairs) for value in values]
    return [combine(*both) for combine, *both in zip(combines, values, others)]


def over_plane(values, combines):
    for axis in ("c", "b", "a"):
        values = pairwise(values, combines, axis, [(0, 1), (1, 0)])
    return values


def over_trees(values, combines):
    count = lax.axis_size(TREE)
    hop = 1
    while hop < count:
        values = pairwise(values, combines, TREE, [(i, i ^ hop) for i in range(count)])
        hop *= 2
    return values


def tree_tables(lengths, parent_row):
    count = lengths.shape[0]
    numbers = jnp.arange(count, dtype=jnp.int32)
    ends = jnp.sum(jnp.where(numbers[None, :] <= numbers[:, None], lengths[None, :], 0), axis=1)
    starts = ends - lengths
    reach = (
        (numbers[:, None] == numbers[None, :]) | (parent_row[:, None] == numbers[None, :])
    ).astype(F32)
    hops = 1
    while hops < count:
        reach = (
            jnp.sum(reach[:, :, None] * reach[None, :, :], axis=1) > 0.5
        ).astype(F32)
        hops *= 2
    return starts, ends, reach


def block_lists(hot, path, q_blocks, k_blocks):
    q_has = jnp.max(path.reshape(q_blocks, -1, path.shape[1]), axis=1)
    k_has = jnp.max(hot.reshape(k_blocks, -1, hot.shape[1]), axis=1)
    live = jnp.sum(q_has[:, None, :] * k_has[None, :, :], axis=2) > 0.5
    q_first = jnp.arange(q_blocks, dtype=jnp.int32) * (BQ // BK)
    keys = jnp.arange(k_blocks, dtype=jnp.int32)
    live = (live & (keys[None, :] < q_first[:, None])).astype(jnp.int32)
    rank = jnp.sum(
        jnp.where(keys[None, :, None] > keys[None, None, :], live[:, None, :], 0), axis=2
    )
    listed = jnp.sum(
        jnp.where(
            (rank[:, :, None] == keys[None, None, :]) & (live[:, :, None] > 0),
            keys[None, :, None],
            0,
        ),
        axis=1,
    )
    return jnp.sum(live, axis=1).astype(jnp.int32), listed.astype(jnp.int32)


def score_block(kx, qx):
    return lax.dot_general(kx, qx, (((1,), (1,)), ((), ())), preferred_element_type=F32)


def causal(key_first, query_first):
    keys = key_first + lax.broadcasted_iota(jnp.int32, (BK, BQ), 0)
    queries = query_first + lax.broadcasted_iota(jnp.int32, (BK, BQ), 1)
    return keys <= queries


def in_blocks(count, listed, step, group, some):
    others = count[step]

    @pl.when(others % 2 == 0)
    def _():
        for h in group:
            some(h, (step,), True)

    @pl.when(others % 2 == 1)
    def _():
        for h in group:
            some(h, (step, listed[step, others - 1]), True)

    pairs = others // 2

    @pl.when(pairs % 2 == 1)
    def _():
        for h in group:
            some(h, (listed[step, 2 * pairs - 2], listed[step, 2 * pairs - 1]), False)

    def body(i, carry):
        for h in group:
            some(h, tuple(listed[step, 4 * i + k] for k in range(4)), False)
        return carry

    lax.fori_loop(0, pairs // 2, body, 0)


def head_cols(part, h, local):
    at = (part * local + h) * HEAD_DIM
    return slice(at, at + HEAD_DIM)


def attend_kernel(
    count, listed, owned, proj, q_mark, k_mark, out, out_wide, lse, top, kx, vt, qx, m_s, l_s, acc_s
):
    step = pl.program_id(0)
    q_first = step * BQ
    local = acc_s.shape[0]
    here = pl.ds(pl.multiple_of(q_first, BQ), BQ)

    @pl.when(step == 0)
    def _():
        top[...] = jnp.full(top.shape, NEGATIVE, F32)

    for h in range(local):
        kx[h, here, :] = jnp.concatenate([proj[:, head_cols(1, h, local)], k_mark[...]], axis=1)
        query = proj[:, head_cols(0, h, local)] * jnp.asarray(HEAD_DIM ** (-0.5), BF)
        qx[h] = jnp.concatenate([query, q_mark[...]], axis=1)
    vt[:, here] = proj[:, 2 * local * HEAD_DIM :].T

    def some(h, blocks, diagonal):
        rows = [pl.ds(pl.multiple_of(kb * BK, BK), BK) for kb in blocks]
        scores = [score_block(kx[h, r, :], qx[h]) for r in rows]
        if diagonal:
            scores[0] = jnp.where(causal(blocks[0] * BK, q_first), scores[0], NEGATIVE)
        old = m_s[h : h + 1, :]
        new = old
        for score in scores:
            new = jnp.maximum(new, jnp.max(score, axis=0, keepdims=True))
        weights = [jnp.exp(score - new) for score in scores]
        shrink = jnp.exp(old - new)
        m_s[h : h + 1, :] = new
        l_s[h : h + 1, :] = l_s[h : h + 1, :] * shrink + sum(
            jnp.sum(weight, axis=0, keepdims=True) for weight in weights
        )
        acc_s[h] = acc_s[h] * shrink + sum(
            jnp.dot(
                vt[h * HEAD_DIM : (h + 1) * HEAD_DIM, r],
                weight.astype(BF),
                preferred_element_type=F32,
            )
            for r, weight in zip(rows, weights)
        )

    def heads(group):
        for h in group:
            m_s[h : h + 1, :] = jnp.full((1, BQ), NEGATIVE, F32)
            l_s[h : h + 1, :] = jnp.zeros((1, BQ), F32)
            acc_s[h] = jnp.zeros((HEAD_DIM, BQ), F32)
        in_blocks(count, listed, step, group, some)
        for h in group:
            total = l_s[h : h + 1, :]
            out_wide[h] = acc_s[h] / total
            lse[h : h + 1, :] = m_s[h : h + 1, :] + jnp.log(total)
            top[h : h + 1, :] = jnp.maximum(top[h : h + 1, :], m_s[h : h + 1, :])

    last = local - 1
    heads(range(last))

    @pl.when(owned[step] > 0)
    def _():
        heads([last])

    @pl.when(owned[step] == 0)
    def _():
        out_wide[last] = jnp.zeros((HEAD_DIM, BQ), F32)
        lse[last : last + 1, :] = jnp.zeros((1, BQ), F32)

    for h in range(local):
        out[:, h * HEAD_DIM : (h + 1) * HEAD_DIM] = out_wide[h].T.astype(BF)


def whole_block(shape):
    return pl.BlockSpec(shape, lambda i, *_: (0,) * len(shape), pipeline_mode=pl.Buffered(1))


def attend(count, listed, owned, proj, q_mark, k_mark):
    tokens, width = proj.shape
    heads = width // (3 * HEAD_DIM)
    return pl.pallas_call(
        attend_kernel,
        grid_spec=pltpu.PrefetchScalarGridSpec(
            num_scalar_prefetch=3,
            grid=(tokens // BQ,),
            in_specs=[
                pl.BlockSpec((BQ, width), lambda i, *_: (i, 0)),
                pl.BlockSpec((BQ, q_mark.shape[1]), lambda i, *_: (i, 0)),
                pl.BlockSpec((BQ, k_mark.shape[1]), lambda i, *_: (i, 0)),
            ],
            out_specs=[
                pl.BlockSpec((BQ, heads * HEAD_DIM), lambda i, *_: (i, 0)),
                pl.BlockSpec((heads, HEAD_DIM, BQ), lambda i, *_: (0, 0, i)),
                pl.BlockSpec((heads, BQ), lambda i, *_: (0, i)),
                pl.BlockSpec((heads, BQ), lambda i, *_: (0, 0)),
            ],
            scratch_shapes=[
                pltpu.VMEM((heads, tokens, LANES), BF),
                pltpu.VMEM((heads * HEAD_DIM, tokens), BF),
                pltpu.VMEM((heads, BQ, LANES), BF),
                pltpu.VMEM((heads, BQ), F32),
                pltpu.VMEM((heads, BQ), F32),
                pltpu.VMEM((heads, HEAD_DIM, BQ), F32),
            ],
        ),
        out_shape=[
            jax.ShapeDtypeStruct((tokens, heads * HEAD_DIM), BF),
            jax.ShapeDtypeStruct((heads, HEAD_DIM, tokens), F32),
            jax.ShapeDtypeStruct((heads, tokens), F32),
            jax.ShapeDtypeStruct((heads, BQ), F32),
        ],
        compiler_params=pltpu.CompilerParams(
            dimension_semantics=("arbitrary",), vmem_limit_bytes=32 << 20
        ),
        cost_estimate=pl.CostEstimate(
            flops=heads * tokens * tokens * HEAD_DIM * 4,
            bytes_accessed=heads * tokens * 1024,
            transcendentals=heads * tokens * tokens // 2,
        ),
        name="attend",
    )(count, listed, owned, proj, q_mark, k_mark)


def attend_back_kernel(
    count, listed, owned, proj, q_mark, k_mark, up, out_wide, lse, grads, kx, kt, vs, qx, dk_s, dv_s, dq_s
):
    step = pl.program_id(0)
    q_first = step * BQ
    local = dq_s.shape[0]
    last = local - 1
    width = local * HEAD_DIM
    here = pl.ds(pl.multiple_of(q_first, BQ), BQ)

    for h in range(local):
        kx[h, here, :] = jnp.concatenate([proj[:, head_cols(1, h, local)], k_mark[...]], axis=1)
        query = proj[:, head_cols(0, h, local)] * jnp.asarray(HEAD_DIM ** (-0.5), BF)
        qx[h] = jnp.concatenate([query, q_mark[...]], axis=1)
        vs[h, here, :] = proj[:, head_cols(2, h, local)]
        dk_s[h, here, :] = jnp.zeros((BQ, HEAD_DIM), F32)
        dv_s[h, here, :] = jnp.zeros((BQ, HEAD_DIM), F32)
    kt[:, here] = proj[:, width : 2 * width].T

    def heads(group):
        parts = {}
        for h in group:
            rows_up = up[:, h * HEAD_DIM : (h + 1) * HEAD_DIM]
            cols_up = rows_up.astype(F32).T
            delta = jnp.sum(out_wide[h] * cols_up, axis=0, keepdims=True)
            parts[h] = (rows_up, cols_up.astype(BF), delta, lse[h : h + 1, :])
            dq_s[h] = jnp.zeros((HEAD_DIM, BQ), F32)

        def some(h, blocks, diagonal):
            rows_up, cols_up, delta, norm = parts[h]
            rows = [pl.ds(pl.multiple_of(kb * BK, BK), BK) for kb in blocks]
            probs = [jnp.exp(score_block(kx[h, r, :], qx[h]) - norm) for r in rows]
            if diagonal:
                probs[0] = jnp.where(causal(blocks[0] * BK, q_first), probs[0], 0.0)
            dprobs = [jnp.dot(vs[h, r, :], cols_up, preferred_element_type=F32) for r in rows]
            dscores = [(p * (d - delta)).astype(BF) for p, d in zip(probs, dprobs)]
            for r, p, d in zip(rows, probs, dscores):
                dv_s[h, r, :] += jnp.dot(p.astype(BF), rows_up, preferred_element_type=F32)
                dk_s[h, r, :] += jnp.dot(d, qx[h][:, :HEAD_DIM], preferred_element_type=F32)
            dq_s[h] += sum(
                jnp.dot(
                    kt[h * HEAD_DIM : (h + 1) * HEAD_DIM, r], d, preferred_element_type=F32
                )
                for r, d in zip(rows, dscores)
            )

        in_blocks(count, listed, step, group, some)

    heads(range(last))

    @pl.when(owned[step] > 0)
    def _():
        heads([last])

    @pl.when(owned[step] == 0)
    def _():
        dq_s[last] = jnp.zeros((HEAD_DIM, BQ), F32)

    for h in range(local):
        grads[here, h * HEAD_DIM : (h + 1) * HEAD_DIM] = (
            dq_s[h] * (HEAD_DIM ** (-0.5))
        ).T.astype(BF)

    @pl.when(step == pl.num_programs(0) - 1)
    def _():
        for h in range(local):
            at = width + h * HEAD_DIM
            grads[:, at : at + HEAD_DIM] = dk_s[h].astype(BF)
            at = 2 * width + h * HEAD_DIM
            grads[:, at : at + HEAD_DIM] = dv_s[h].astype(BF)


def attend_back(count, listed, owned, proj, q_mark, k_mark, up, out_wide, lse):
    tokens, width = proj.shape
    heads = width // (3 * HEAD_DIM)
    return pl.pallas_call(
        attend_back_kernel,
        grid_spec=pltpu.PrefetchScalarGridSpec(
            num_scalar_prefetch=3,
            grid=(tokens // BQ,),
            in_specs=[
                pl.BlockSpec((BQ, width), lambda i, *_: (i, 0)),
                pl.BlockSpec((BQ, q_mark.shape[1]), lambda i, *_: (i, 0)),
                pl.BlockSpec((BQ, k_mark.shape[1]), lambda i, *_: (i, 0)),
                pl.BlockSpec((BQ, heads * HEAD_DIM), lambda i, *_: (i, 0)),
                pl.BlockSpec((heads, HEAD_DIM, BQ), lambda i, *_: (0, 0, i)),
                pl.BlockSpec((heads, BQ), lambda i, *_: (0, i)),
            ],
            out_specs=whole_block((tokens, width)),
            scratch_shapes=[
                pltpu.VMEM((heads, tokens, LANES), BF),
                pltpu.VMEM((heads * HEAD_DIM, tokens), BF),
                pltpu.VMEM((heads, tokens, HEAD_DIM), BF),
                pltpu.VMEM((heads, BQ, LANES), BF),
                pltpu.VMEM((heads, tokens, HEAD_DIM), F32),
                pltpu.VMEM((heads, tokens, HEAD_DIM), F32),
                pltpu.VMEM((heads, HEAD_DIM, BQ), F32),
            ],
        ),
        out_shape=jax.ShapeDtypeStruct((tokens, width), BF),
        compiler_params=pltpu.CompilerParams(
            dimension_semantics=("arbitrary",), vmem_limit_bytes=44 << 20
        ),
        cost_estimate=pl.CostEstimate(
            flops=heads * tokens * tokens * HEAD_DIM * 10,
            bytes_accessed=heads * tokens * 2048,
            transcendentals=heads * tokens * tokens // 2,
        ),
        name="attend_back",
    )(count, listed, owned, proj, q_mark, k_mark, up, out_wide, lse)


def head_split(matrix, parts):
    rows, cols = matrix.shape
    heads = cols // (parts * HEAD_DIM)
    each = heads // GROUP
    cube = matrix.reshape(rows, parts, heads, HEAD_DIM)
    own = cube[:, :, : each * GROUP].reshape(rows, parts, GROUP, each, HEAD_DIM)
    rest = jnp.broadcast_to(
        cube[:, :, None, each * GROUP :], (rows, parts, GROUP, heads - each * GROUP, HEAD_DIM)
    )
    joined = jnp.concatenate([own, rest], axis=3)
    return jnp.transpose(joined, (2, 0, 1, 3, 4)).reshape(GROUP, rows, -1)


def head_join(shares, parts, heads):
    group, rows, _ = shares.shape
    each = heads // GROUP
    cube = shares.astype(F32).reshape(group, rows, parts, -1, HEAD_DIM)
    own = jnp.transpose(cube[:, :, :, :each], (1, 2, 0, 3, 4)).reshape(
        rows, parts, each * GROUP, HEAD_DIM
    )
    rest = jnp.sum(cube[:, :, :, each:], axis=0)
    return jnp.concatenate([own, rest], axis=2).reshape(rows, -1)


def hidden_split(matrix, unit):
    rows = matrix.shape[0]
    cube = matrix.reshape(rows, -1, GROUP, unit)
    return jnp.transpose(cube, (2, 0, 1, 3)).reshape(GROUP, rows, -1)


def hidden_join(shares, unit):
    group, rows, _ = shares.shape
    cube = shares.reshape(group, rows, -1, unit)
    return jnp.transpose(cube, (1, 2, 0, 3)).reshape(rows, -1)


def exchange(shares):
    return lax.all_to_all(shares, PLANE, split_axis=0, concat_axis=0, tiled=True)


def take(stack, place):
    return lax.dynamic_index_in_dim(stack, place, 0, keepdims=False)


def columns_start(shard, width, split):
    if shard.size % width == 0:
        mine = exchange(split(shard.reshape(-1, width)))
        return mine.reshape(-1, mine.shape[-1])
    return shard


def columns_end(rows, size, width, split, place):
    if size % width == 0:
        return lax.all_gather(rows, TREE, axis=0, tiled=True)
    full = lax.all_gather(rows, EVERY, axis=0, tiled=True).reshape(-1, width)
    return take(split(full), place)


def columns_first(grad, size, width):
    if size % width == 0:
        rows = lax.psum_scatter(grad, TREE, scatter_dimension=0, tiled=True)
        return rows.reshape(GROUP, -1, rows.shape[-1])
    return grad


def columns_second(slots, join, shard_shape, width, place):
    if shard_shape[0] * shard_shape[1] % width == 0:
        return join(slots).astype(F32).reshape(shard_shape)
    spots = jnp.arange(GROUP, dtype=jnp.int32)[:, None, None] == place
    shares = jnp.where(spots, slots[None], jnp.zeros((), BF))
    full = join(shares).astype(BF).reshape(-1, shard_shape[1])
    return lax.psum_scatter(full, EVERY, scatter_dimension=0, tiled=True).astype(F32)


def owner_rows(share, trees):
    t, p, i = (
        lax.broadcasted_iota(jnp.int32, (trees, GROUP, share), dim) for dim in range(3)
    )
    return (t * GROUP + p) * share + i


def slots_out(columns, own, share, place):
    rows = owner_rows(share, lax.axis_size(TREE)) - place * own
    numbers = jnp.arange(own, dtype=jnp.int32)
    pick = jnp.any(rows[..., None] == numbers, axis=0).reshape(-1, own).astype(BF)
    slots = lax.dot_general(
        pick, columns[:, :own], (((1,), (1,)), ((), ())), preferred_element_type=F32
    )
    return slots.astype(BF).reshape(GROUP, share, -1)


def slots_in(slots, own, share, place, padded):
    trees = lax.axis_size(TREE)
    rows = take(jnp.swapaxes(owner_rows(share, trees), 0, 1), place)
    total = jnp.zeros((trees,) + slots.shape[1:], slots.dtype)
    for source in range(GROUP):
        held = (rows >= source * own) & (rows < (source + 1) * own)
        total = jnp.where(held[:, :, None], slots[source][None], total)
    return jnp.pad(total, ((0, 0), (0, padded - share), (0, 0))).reshape(trees * padded, -1)


def on_device(
    tokens,
    cotangent,
    w_qkv,
    w_out,
    w_fc,
    w_proj,
    ln1_gain,
    ln1_bias,
    q_bias,
    v_bias,
    out_bias,
    ln2_gain,
    ln2_bias,
    fc_bias,
    proj_bias,
    seg_lengths,
    parents,
):
    tok_dev, model_width = tokens.shape
    hidden = fc_bias.shape[0]
    flat_cols = w_qkv.shape[1]
    heads = model_width // HEAD_DIM
    each = heads // GROUP
    rest = heads - each * GROUP
    local = each + rest
    tree = lax.axis_index(TREE)
    place = (lax.axis_index("a") * 2 + lax.axis_index("b")) * 2 + lax.axis_index("c")
    device = tree * GROUP + place
    unit = max(1, hidden // lax.axis_size(EVERY))

    starts, ends, reach = tree_tables(take(seg_lengths, tree), take(parents, tree))
    position = jnp.arange(TREE_TOK, dtype=jnp.int32)
    hot = (
        (position[:, None] >= starts[None, :]) & (position[:, None] < ends[None, :])
    ).astype(F32)
    path = jnp.dot(hot, reach, preferred_element_type=F32)
    q_blocks, k_blocks = TREE_TOK // BQ, TREE_TOK // BK
    count, listed = block_lists(hot, path, q_blocks, k_blocks)
    block_numbers = jnp.arange(q_blocks, dtype=jnp.int32)
    turn = q_blocks - 1 - block_numbers
    owner = jnp.where(turn < GROUP, turn, 2 * GROUP - 2 - turn)
    owned = (owner == place).astype(jnp.int32)
    pad = LANES - HEAD_DIM - hot.shape[1]
    k_mark = jnp.pad(hot, ((0, 0), (0, pad))).astype(BF)
    q_mark = jnp.pad((1.0 - path) * NEGATIVE, ((0, 0), (0, pad))).astype(BF)

    residual_in = tokens.astype(F32)
    first_norm, normed_one, inv_one = norm_forward(residual_in, ln1_gain, ln1_bias)
    first_own = first_norm.astype(BF)
    qkv_split, fc_split = partial(head_split, parts=3), partial(hidden_split, unit=unit)
    qkv_rows = columns_start(w_qkv, 3 * model_width, qkv_split)
    w_qkv_l = columns_end(qkv_rows, w_qkv.size, 3 * model_width, qkv_split, place)
    qkv_bias = jnp.concatenate([q_bias, jnp.zeros_like(q_bias), v_bias])
    qkv_bias_l = take(head_split(qkv_bias[None], 3), place)[0]
    first_low, _ = plane_gather(first_own, place)

    two_near = plane_near(after(cotangent, first_low))
    whole_rows = w_out.size % model_width == 0
    ratio = model_width // flat_cols
    w_out_full = lax.all_gather(after(w_out, first_low), EVERY, axis=0, tiled=True)
    w_out_l = jnp.concatenate(
        [
            block_of(w_out_full, place, each * HEAD_DIM * ratio),
            w_out_full[each * GROUP * HEAD_DIM * ratio :],
        ],
        axis=0,
    ).reshape(-1, model_width)
    proj_whole = w_proj.size % model_width == 0
    if proj_whole:
        w_proj_l = lax.all_gather(
            after(w_proj.reshape(-1, model_width), first_low), TREE, axis=0, tiled=True
        )
    else:
        proj_full = lax.all_gather(w_proj, EVERY, axis=0, tiled=True).reshape(hidden, model_width)
        w_proj_l = take(
            jnp.transpose(proj_full.reshape(-1, GROUP, unit, model_width), (1, 0, 2, 3)), place
        ).reshape(-1, model_width)
    fc_bias_l = take(hidden_split(fc_bias[None], unit), place)[0]
    projected = (jnp.dot(first_low, w_qkv_l, preferred_element_type=F32) + qkv_bias_l).astype(BF)

    fc_rows = columns_start(after(w_fc, projected), hidden, fc_split)
    attended, out_wide, lse, tops = attend(count, listed, owned, projected, q_mark, k_mark)
    attended, two_near, fc_rows = lax.optimization_barrier((attended, two_near, fc_rows))
    two_far = plane_far(*two_near)
    attended = after(attended, two_far)
    w_fc_l = columns_end(fc_rows, w_fc.size, hidden, fc_split, place)
    branch = jnp.dot(attended, w_out_l, preferred_element_type=F32).astype(BF)
    mid_sum, mid_last = plane_scatter(branch, place)
    two_blocks = after((cotangent, *two_near, two_far), *mid_last)
    grad_two = plane_write(two_blocks, [swap(block, "c") for block in two_blocks], place, None)
    middle = residual_in + mid_sum + out_bias

    second_norm, normed_two, inv_two = norm_forward(middle, ln2_gain, ln2_bias)
    second_own = second_norm.astype(BF)
    second_low, _ = plane_gather(second_own, place, branch)
    own_slots = ()
    if whole_rows:
        share = w_out.size // model_width
        own_slots = slots_out(after(attended, second_own), each * HEAD_DIM, share, place)
        own_slots = exchange(after(own_slots, second_low))
    pre_act = jnp.dot(second_low, w_fc_l, preferred_element_type=F32) + fc_bias_l
    activated, gelu_pull = jax.vjp(partial(jax.nn.gelu, approximate=True), pre_act)
    act_low = activated.astype(BF)
    over_cols = lambda left, right: lax.dot_general(
        left, right, (((1,), (1,)), ((), ())), preferred_element_type=F32
    )
    over_rows = lambda left, right: lax.dot_general(
        left, right, (((0,), (0,)), ((), ())), preferred_element_type=F32
    )
    pre_low = gelu_pull(over_cols(grad_two, w_proj_l))[0].astype(BF)
    norm_back = over_cols(pre_low, w_fc_l).astype(BF)
    norm_back, own_slots = lax.optimization_barrier((norm_back, own_slots))
    back_sum, back_last = plane_scatter(norm_back, place)

    grad_out = cotangent.astype(F32)
    proj_bias_grad = jnp.sum(grad_out, axis=0)
    mid_part, ln2_gain_grad, ln2_bias_grad = norm_backward(back_sum, normed_two, inv_two, ln2_gain)
    middle_grad = grad_out + mid_part
    branch_own = middle_grad.astype(BF)
    out_bias_grad = jnp.sum(branch_own.astype(F32), axis=0)

    branch_low, _ = plane_gather(branch_own, place, norm_back)

    fc_low = over_rows(second_low, after(pre_low, branch_own)).astype(BF)
    proj_low = over_rows(after(act_low, branch_own), grad_two).astype(BF)
    branch_two = jnp.dot(
        after(act_low, proj_low), w_proj_l, preferred_element_type=F32
    ).astype(BF)
    attn_back = over_cols(branch_low, w_out_l).astype(BF)
    attn_back = after(attn_back, branch_two)

    two_sum = lax.psum_scatter(
        after(branch_two, branch_low), PLANE, scatter_dimension=0, tiled=True
    )
    fc_rows = columns_first(fc_low, w_fc.size, hidden)
    proj_parts = tree_parts(proj_low) if proj_whole else ()
    qkv_low = attend_back(
        count, listed, owned, projected, q_mark, k_mark, attn_back, out_wide, lse
    )
    qkv_low, fc_rows, proj_parts = lax.optimization_barrier((qkv_low, fc_rows, proj_parts))
    if w_fc.size % hidden == 0:
        fc_rows = exchange(fc_rows)
    first_back = over_cols(qkv_low, w_qkv_l).astype(BF)
    made = []

    def beside(sent):
        made.append(over_rows(first_low, after(qkv_low, two_sum, *sent)).astype(BF))
        return made + [fc_rows]

    in_sum, in_last = plane_scatter(first_back, place, beside)
    qkv_rows = columns_first(made[0], w_qkv.size, 3 * model_width)
    branch_late = after(branch_low, *in_last)
    if whole_rows:
        padded = -(-share // 16) * 16
        out_rows = jnp.dot(
            slots_in(after(own_slots, *in_last), each * HEAD_DIM, share, place, padded),
            branch_late,
            preferred_element_type=F32,
        ).astype(BF)
        out_rows = lax.psum_scatter(
            after(out_rows, qkv_rows), TREE, scatter_dimension=0, tiled=True
        )
        common = over_rows(attended[:, each * HEAD_DIM :], branch_late).astype(BF)
    else:
        out_low = over_rows(attended, branch_late).astype(BF)
        common = jnp.zeros((8, LANES), BF)
    in_part, ln1_gain_grad, ln1_bias_grad = norm_backward(in_sum, normed_one, inv_one, ln1_gain)

    fc_bias_part = jnp.sum(after(pre_low, *in_last).astype(F32), axis=0)
    fc_parts = jnp.zeros((GROUP, hidden // GROUP), F32)
    fc_parts = lax.dynamic_update_slice(fc_parts, fc_bias_part[None], (place, 0))
    fc_parts = hidden_join(fc_parts[:, None], unit)[0]
    column_sums = jnp.sum(after(qkv_low, *in_last).astype(F32), axis=0)
    column_sums = column_sums.reshape(3, local, HEAD_DIM)
    bias_parts = jnp.zeros((3, GROUP, each, HEAD_DIM), F32)
    bias_parts = lax.dynamic_update_slice(
        bias_parts, column_sums[:, None, :each], (0, place, 0, 0)
    )
    bias_parts = jnp.concatenate(
        [bias_parts.reshape(3, each * GROUP, HEAD_DIM), column_sums[:, each:]], axis=1
    ).reshape(3, model_width)
    sums = jnp.concatenate(
        [
            ln1_gain_grad,
            ln1_bias_grad,
            bias_parts[0],
            bias_parts[2],
            out_bias_grad,
            ln2_gain_grad,
            ln2_bias_grad,
            proj_bias_grad,
            fc_parts,
        ]
    )
    top_heads = jnp.max(tops, axis=1)
    spread = jnp.full((GROUP, each), NEGATIVE, F32)
    spread = lax.dynamic_update_slice(spread, top_heads[None, :each], (place, 0))
    spread = jnp.concatenate([spread.reshape(-1), top_heads[each:]])
    is_sum = jnp.arange(sums.shape[0] + heads, dtype=jnp.int32) < sums.shape[0]
    combine = lambda left, right: jnp.where(is_sum, left + right, jnp.maximum(left, right))
    sums = jnp.concatenate([sums, spread])

    whole_qkv = w_qkv.size % (3 * model_width) == 0
    add = lambda left, right: left + right
    combines = [combine, add]
    (common,) = over_trees([common], [add])
    sums, common = over_plane(lax.optimization_barrier((sums, common)), combines)
    if whole_qkv:
        qkv_rows = exchange(after(qkv_rows, in_sum))
    sums, common, qkv_rows = lax.optimization_barrier((sums, common, qkv_rows))
    (sums,) = over_trees([sums], [combine])
    logit_max = sums[-heads:]
    qkv_shard = columns_second(
        qkv_rows, partial(head_join, parts=3, heads=heads), w_qkv.shape, 3 * model_width, place
    )
    fc_shard = columns_second(
        after(fc_rows, sums), partial(hidden_join, unit=unit), w_fc.shape, hidden, place
    )
    if whole_rows:
        rows = device * share + jnp.arange(share, dtype=jnp.int32) - GROUP * each * HEAD_DIM
        numbers = jnp.arange(common.shape[0], dtype=jnp.int32)
        pick = (rows[:, None] == numbers[None, :]).astype(BF)
        out_shard = out_rows[:share].astype(F32) + jnp.dot(
            pick, common, preferred_element_type=F32
        )
        out_shard = out_shard.reshape(w_out.shape)
    else:
        out_zero = jnp.zeros((each * GROUP * HEAD_DIM, model_width), BF)
        out_rows = jnp.concatenate(
            [
                lax.dynamic_update_slice(
                    out_zero, out_low[: each * HEAD_DIM], (place * each * HEAD_DIM, 0)
                ),
                out_low[each * HEAD_DIM :],
            ],
            axis=0,
        ).reshape(-1, flat_cols)
        out_shard = lax.psum_scatter(out_rows, EVERY, scatter_dimension=0, tiled=True).astype(F32)
    if proj_whole:
        proj_shard = sum(part.astype(F32) for part in after(proj_parts, in_sum))
        proj_shard = proj_shard.reshape(w_proj.shape)
    else:
        spots = jnp.arange(GROUP, dtype=jnp.int32)[None, :, None, None] == place
        proj_rows = jnp.where(
            spots, proj_low.reshape(-1, 1, unit, model_width), jnp.zeros((), BF)
        ).reshape(-1, flat_cols)
        proj_shard = lax.psum_scatter(proj_rows, EVERY, scatter_dimension=0, tiled=True).astype(F32)
    input_grad = middle_grad + in_part
    output = (middle + after(two_sum, sums).astype(F32) + proj_bias).astype(BF)

    cut = lambda array, i: array[i * model_width : (i + 1) * model_width]
    small = (
        *(cut(sums, i) for i in range(7)),
        sums[8 * model_width : -heads],
        cut(sums, 7),
    )

    clip_gain = jnp.sqrt(TAU / jnp.maximum(logit_max, TAU))
    rows_dev = w_qkv.shape[0]
    flat_index = (after(device, in_sum) * rows_dev + jnp.arange(rows_dev, dtype=jnp.int32)[:, None]) * flat_cols
    flat_index = flat_index + jnp.arange(flat_cols, dtype=jnp.int32)[None, :]
    column = flat_index % (3 * model_width)
    head_of = column % model_width // HEAD_DIM
    head_numbers = jnp.arange(heads, dtype=jnp.int32)
    head_gain = jnp.sum(
        jnp.where(
            head_of[:, :, None] == head_numbers[None, None, :], clip_gain[None, None, :], 0.0
        ),
        axis=2,
    )
    factor = jnp.where(column < 2 * model_width, head_gain, 1.0)
    clipped = (w_qkv.astype(F32) * factor).astype(BF)
    return (
        output,
        input_grad,
        qkv_shard,
        out_shard,
        fc_shard,
        proj_shard,
        *small,
        logit_max,
        clipped,
    )


def solution(mesh):
    split = Mesh(mesh.devices.reshape(-1, 2, 2, 2), EVERY)
    rows = P(EVERY, None)
    return jax.shard_map(
        on_device,
        mesh=split,
        in_specs=(rows,) * 6 + (P(),) * 11,
        out_specs=(rows,) * 6 + (P(),) * 10 + (rows,),
        check_vma=False,
    )
```

```python
from functools import partial

import jax
import jax.numpy as jnp
from jax import lax
from jax.experimental import pallas as pl
from jax.experimental.layout import Layout, with_layout_constraint
from jax.experimental.pallas import tpu as pltpu
from jax.sharding import Mesh, PartitionSpec as P

HEAD_DIM = 64
TREE_TOK = 2560
GROUP = 8

EPS = 1e-05
TAU = 7.0
NEGATIVE = -1e30

BQ = 256
BK = 256
LANES = 128

TREE = "t"
PLANE = ("a", "b", "c")
EVERY = ("t", "a", "b", "c")
BF = jnp.bfloat16
F32 = jnp.float32


def norm_forward(values, norm_gain, norm_shift):
    row_mean = jnp.mean(values, axis=-1, keepdims=True)
    centered = values - row_mean
    inv_std = lax.rsqrt(jnp.mean(centered * centered, axis=-1, keepdims=True) + EPS)
    normed = centered * inv_std
    return (normed * norm_gain + norm_shift, normed, inv_std)


def norm_backward(upstream, normed, inv_std, norm_gain):
    scaled = upstream * norm_gain
    inner = (
        scaled
        - jnp.mean(scaled, axis=-1, keepdims=True)
        - normed * jnp.mean(scaled * normed, axis=-1, keepdims=True)
    )
    return (inner * inv_std, jnp.sum(upstream * normed, axis=0), jnp.sum(upstream, axis=0))


def swap(value, axis):
    return lax.ppermute(value, axis, [(0, 1), (1, 0)])


def after(value, *others):
    return lax.optimization_barrier((value, *others))[0] if others else value


def rows_major(array):
    return with_layout_constraint(array, Layout(major_to_minor=tuple(range(array.ndim))))


def plane_write(blocks, other, place, base):
    rows = blocks[0].shape[0]
    full = base
    if full is None:
        full = jnp.zeros((GROUP * rows,) + blocks[0].shape[1:], blocks[0].dtype)
    for r, block in enumerate(blocks):
        for q, piece in ((2 * r, block), (2 * r + 1, other[r])):
            full = lax.dynamic_update_slice_in_dim(full, piece, (place ^ q) * rows, 0)
    return rows_major(full)


def plane_gather(own, place, base=None):
    half = own.shape[0] // 2
    from_b, from_a = swap(own, "b"), swap(own, "a")
    diag = jnp.concatenate([swap(from_b[:half], "a"), swap(from_a[half:], "b")], axis=0)
    blocks = (own, from_b, from_a, diag)
    full = plane_write(blocks, [swap(block, "c") for block in blocks], place, base)
    return full, (from_b, from_a)


def plane_near(own):
    return swap(own, "b"), swap(own, "a")


def plane_far(from_b, from_a):
    half = from_b.shape[0] // 2
    return jnp.concatenate([swap(from_b[:half], "a"), swap(from_a[half:], "b")], axis=0)


def plane_scatter(array, place, hold=lambda sent: ()):
    rows = array.shape[0] // GROUP
    array = rows_major(array)
    sent = [block_of(array, place ^ r, rows) for r in range(GROUP)]
    sent = list(lax.optimization_barrier(tuple(sent)))
    came = tuple(swap(sent[r + 1], "c") for r in (6, 2, 4, 0))
    came = after(came, *hold(sent))
    diag, for_b, for_a, mine = (
        sent[r].astype(F32) + block.astype(F32) for r, block in zip((6, 2, 4, 0), came)
    )
    half = diag.shape[0] // 2
    top, bottom = lax.optimization_barrier((diag[:half].astype(BF), diag[half:].astype(BF)))
    top, bottom = swap(top, "b"), swap(bottom, "a")
    for_a = jnp.concatenate([for_a[:half] + top.astype(F32), for_a[half:]], axis=0).astype(BF)
    for_b = jnp.concatenate([for_b[:half], for_b[half:] + bottom.astype(F32)], axis=0).astype(BF)
    for_a, for_b = lax.optimization_barrier((for_a, for_b))
    total = mine + swap(for_b, "b").astype(F32) + swap(for_a, "a").astype(F32)
    return total, (for_a, for_b)


def block_of(array, index, rows):
    return lax.dynamic_slice_in_dim(array, index * rows, rows, 0)


def tree_parts(grad):
    count, me = lax.axis_size(TREE), lax.axis_index(TREE)
    rows = grad.shape[0] // count
    parts = [block_of(grad, me, rows)]
    for hop in range(1, count):
        sent = block_of(grad, (me + hop) % count, rows)
        pairs = [(i, (i + hop) % count) for i in range(count)]
        parts.append(lax.ppermute(sent, TREE, pairs))
    return tuple(parts)


def pairwise(values, combines, axis, pairs):
    others = [lax.ppermute(value, axis, pairs) for value in values]
    return [combine(*both) for combine, *both in zip(combines, values, others)]


def over_plane(values, combines):
    for axis in ("c", "b", "a"):
        values = pairwise(values, combines, axis, [(0, 1), (1, 0)])
    return values


def over_trees(values, combines):
    count = lax.axis_size(TREE)
    hop = 1
    while hop < count:
        values = pairwise(values, combines, TREE, [(i, i ^ hop) for i in range(count)])
        hop *= 2
    return values


def tree_tables(lengths, parent_row):
    count = lengths.shape[0]
    numbers = jnp.arange(count, dtype=jnp.int32)
    ends = jnp.sum(jnp.where(numbers[None, :] <= numbers[:, None], lengths[None, :], 0), axis=1)
    starts = ends - lengths
    reach = (
        (numbers[:, None] == numbers[None, :]) | (parent_row[:, None] == numbers[None, :])
    ).astype(F32)
    hops = 1
    while hops < count:
        reach = (
            jnp.sum(reach[:, :, None] * reach[None, :, :], axis=1) > 0.5
        ).astype(F32)
        hops *= 2
    return starts, ends, reach


def block_lists(hot, path, q_blocks, k_blocks):
    q_has = jnp.max(path.reshape(q_blocks, -1, path.shape[1]), axis=1)
    k_has = jnp.max(hot.reshape(k_blocks, -1, hot.shape[1]), axis=1)
    live = jnp.sum(q_has[:, None, :] * k_has[None, :, :], axis=2) > 0.5
    q_first = jnp.arange(q_blocks, dtype=jnp.int32) * (BQ // BK)
    keys = jnp.arange(k_blocks, dtype=jnp.int32)
    live = (live & (keys[None, :] < q_first[:, None])).astype(jnp.int32)
    rank = jnp.sum(
        jnp.where(keys[None, :, None] > keys[None, None, :], live[:, None, :], 0), axis=2
    )
    listed = jnp.sum(
        jnp.where(
            (rank[:, :, None] == keys[None, None, :]) & (live[:, :, None] > 0),
            keys[None, :, None],
            0,
        ),
        axis=1,
    )
    return jnp.sum(live, axis=1).astype(jnp.int32), listed.astype(jnp.int32)


def score_block(kx, qx):
    return lax.dot_general(kx, qx, (((1,), (1,)), ((), ())), preferred_element_type=F32)


def causal(key_first, query_first):
    keys = key_first + lax.broadcasted_iota(jnp.int32, (BK, BQ), 0)
    queries = query_first + lax.broadcasted_iota(jnp.int32, (BK, BQ), 1)
    return keys <= queries


def in_blocks(count, listed, step, group, some):
    others = count[step]

    @pl.when(others % 2 == 0)
    def _():
        for h in group:
            some(h, (step,), True)

    @pl.when(others % 2 == 1)
    def _():
        for h in group:
            some(h, (step, listed[step, others - 1]), True)

    pairs = others // 2

    @pl.when(pairs % 2 == 1)
    def _():
        for h in group:
            some(h, (listed[step, 2 * pairs - 2], listed[step, 2 * pairs - 1]), False)

    def body(i, carry):
        for h in group:
            some(h, tuple(listed[step, 4 * i + k] for k in range(4)), False)
        return carry

    lax.fori_loop(0, pairs // 2, body, 0)


def head_cols(part, h, local):
    at = (part * local + h) * HEAD_DIM
    return slice(at, at + HEAD_DIM)


def attend_kernel(
    count, listed, owned, proj, q_mark, k_mark, out, out_wide, lse, top, kx, vt, qx, m_s, l_s, acc_s
):
    step = pl.program_id(0)
    q_first = step * BQ
    local = acc_s.shape[0]
    here = pl.ds(pl.multiple_of(q_first, BQ), BQ)

    @pl.when(step == 0)
    def _():
        top[...] = jnp.full(top.shape, NEGATIVE, F32)

    for h in range(local):
        kx[h, here, :] = jnp.concatenate([proj[:, head_cols(1, h, local)], k_mark[...]], axis=1)
        query = proj[:, head_cols(0, h, local)] * jnp.asarray(HEAD_DIM ** (-0.5), BF)
        qx[h] = jnp.concatenate([query, q_mark[...]], axis=1)
    vt[:, here] = proj[:, 2 * local * HEAD_DIM :].T

    def some(h, blocks, diagonal):
        rows = [pl.ds(pl.multiple_of(kb * BK, BK), BK) for kb in blocks]
        scores = [score_block(kx[h, r, :], qx[h]) for r in rows]
        if diagonal:
            scores[0] = jnp.where(causal(blocks[0] * BK, q_first), scores[0], NEGATIVE)
        old = m_s[h : h + 1, :]
        new = old
        for score in scores:
            new = jnp.maximum(new, jnp.max(score, axis=0, keepdims=True))
        weights = [jnp.exp(score - new) for score in scores]
        shrink = jnp.exp(old - new)
        m_s[h : h + 1, :] = new
        l_s[h : h + 1, :] = l_s[h : h + 1, :] * shrink + sum(
            jnp.sum(weight, axis=0, keepdims=True) for weight in weights
        )
        acc_s[h] = acc_s[h] * shrink + sum(
            jnp.dot(
                vt[h * HEAD_DIM : (h + 1) * HEAD_DIM, r],
                weight.astype(BF),
                preferred_element_type=F32,
            )
            for r, weight in zip(rows, weights)
        )

    def heads(group):
        for h in group:
            m_s[h : h + 1, :] = jnp.full((1, BQ), NEGATIVE, F32)
            l_s[h : h + 1, :] = jnp.zeros((1, BQ), F32)
            acc_s[h] = jnp.zeros((HEAD_DIM, BQ), F32)
        in_blocks(count, listed, step, group, some)
        for h in group:
            total = l_s[h : h + 1, :]
            out_wide[h] = acc_s[h] / total
            lse[h : h + 1, :] = m_s[h : h + 1, :] + jnp.log(total)
            top[h : h + 1, :] = jnp.maximum(top[h : h + 1, :], m_s[h : h + 1, :])

    last = local - 1
    heads(range(last))

    @pl.when(owned[step] > 0)
    def _():
        heads([last])

    @pl.when(owned[step] == 0)
    def _():
        out_wide[last] = jnp.zeros((HEAD_DIM, BQ), F32)
        lse[last : last + 1, :] = jnp.zeros((1, BQ), F32)

    for h in range(local):
        out[:, h * HEAD_DIM : (h + 1) * HEAD_DIM] = out_wide[h].T.astype(BF)


def whole_block(shape):
    return pl.BlockSpec(shape, lambda i, *_: (0,) * len(shape), pipeline_mode=pl.Buffered(1))


def attend(count, listed, owned, proj, q_mark, k_mark):
    tokens, width = proj.shape
    heads = width // (3 * HEAD_DIM)
    return pl.pallas_call(
        attend_kernel,
        grid_spec=pltpu.PrefetchScalarGridSpec(
            num_scalar_prefetch=3,
            grid=(tokens // BQ,),
            in_specs=[
                pl.BlockSpec((BQ, width), lambda i, *_: (i, 0)),
                pl.BlockSpec((BQ, q_mark.shape[1]), lambda i, *_: (i, 0)),
                pl.BlockSpec((BQ, k_mark.shape[1]), lambda i, *_: (i, 0)),
            ],
            out_specs=[
                pl.BlockSpec((BQ, heads * HEAD_DIM), lambda i, *_: (i, 0)),
                pl.BlockSpec((heads, HEAD_DIM, BQ), lambda i, *_: (0, 0, i)),
                pl.BlockSpec((heads, BQ), lambda i, *_: (0, i)),
                pl.BlockSpec((heads, BQ), lambda i, *_: (0, 0)),
            ],
            scratch_shapes=[
                pltpu.VMEM((heads, tokens, LANES), BF),
                pltpu.VMEM((heads * HEAD_DIM, tokens), BF),
                pltpu.VMEM((heads, BQ, LANES), BF),
                pltpu.VMEM((heads, BQ), F32),
                pltpu.VMEM((heads, BQ), F32),
                pltpu.VMEM((heads, HEAD_DIM, BQ), F32),
            ],
        ),
        out_shape=[
            jax.ShapeDtypeStruct((tokens, heads * HEAD_DIM), BF),
            jax.ShapeDtypeStruct((heads, HEAD_DIM, tokens), F32),
            jax.ShapeDtypeStruct((heads, tokens), F32),
            jax.ShapeDtypeStruct((heads, BQ), F32),
        ],
        compiler_params=pltpu.CompilerParams(
            dimension_semantics=("arbitrary",), vmem_limit_bytes=32 << 20
        ),
        cost_estimate=pl.CostEstimate(
            flops=heads * tokens * tokens * HEAD_DIM * 4,
            bytes_accessed=heads * tokens * 1024,
            transcendentals=heads * tokens * tokens // 2,
        ),
        name="attend",
    )(count, listed, owned, proj, q_mark, k_mark)


def attend_back_kernel(
    count, listed, owned, proj, q_mark, k_mark, up, out_wide, lse, grads, kx, kt, vs, qx, dk_s, dv_s, dq_s
):
    step = pl.program_id(0)
    q_first = step * BQ
    local = dq_s.shape[0]
    last = local - 1
    width = local * HEAD_DIM
    here = pl.ds(pl.multiple_of(q_first, BQ), BQ)

    for h in range(local):
        kx[h, here, :] = jnp.concatenate([proj[:, head_cols(1, h, local)], k_mark[...]], axis=1)
        query = proj[:, head_cols(0, h, local)] * jnp.asarray(HEAD_DIM ** (-0.5), BF)
        qx[h] = jnp.concatenate([query, q_mark[...]], axis=1)
        vs[h, here, :] = proj[:, head_cols(2, h, local)]
        dk_s[h, here, :] = jnp.zeros((BQ, HEAD_DIM), F32)
        dv_s[h, here, :] = jnp.zeros((BQ, HEAD_DIM), F32)
    kt[:, here] = proj[:, width : 2 * width].T

    def heads(group):
        parts = {}
        for h in group:
            rows_up = up[:, h * HEAD_DIM : (h + 1) * HEAD_DIM]
            cols_up = rows_up.astype(F32).T
            delta = jnp.sum(out_wide[h] * cols_up, axis=0, keepdims=True)
            parts[h] = (rows_up, cols_up.astype(BF), delta, lse[h : h + 1, :])
            dq_s[h] = jnp.zeros((HEAD_DIM, BQ), F32)

        def some(h, blocks, diagonal):
            rows_up, cols_up, delta, norm = parts[h]
            rows = [pl.ds(pl.multiple_of(kb * BK, BK), BK) for kb in blocks]
            probs = [jnp.exp(score_block(kx[h, r, :], qx[h]) - norm) for r in rows]
            if diagonal:
                probs[0] = jnp.where(causal(blocks[0] * BK, q_first), probs[0], 0.0)
            dprobs = [jnp.dot(vs[h, r, :], cols_up, preferred_element_type=F32) for r in rows]
            dscores = [(p * (d - delta)).astype(BF) for p, d in zip(probs, dprobs)]
            for r, p, d in zip(rows, probs, dscores):
                dv_s[h, r, :] += jnp.dot(p.astype(BF), rows_up, preferred_element_type=F32)
                dk_s[h, r, :] += jnp.dot(d, qx[h][:, :HEAD_DIM], preferred_element_type=F32)
            dq_s[h] += sum(
                jnp.dot(
                    kt[h * HEAD_DIM : (h + 1) * HEAD_DIM, r], d, preferred_element_type=F32
                )
                for r, d in zip(rows, dscores)
            )

        in_blocks(count, listed, step, group, some)

    heads(range(last))

    @pl.when(owned[step] > 0)
    def _():
        heads([last])

    @pl.when(owned[step] == 0)
    def _():
        dq_s[last] = jnp.zeros((HEAD_DIM, BQ), F32)

    for h in range(local):
        grads[here, h * HEAD_DIM : (h + 1) * HEAD_DIM] = (
            dq_s[h] * (HEAD_DIM ** (-0.5))
        ).T.astype(BF)

    @pl.when(step == pl.num_programs(0) - 1)
    def _():
        for h in range(local):
            at = width + h * HEAD_DIM
            grads[:, at : at + HEAD_DIM] = dk_s[h].astype(BF)
            at = 2 * width + h * HEAD_DIM
            grads[:, at : at + HEAD_DIM] = dv_s[h].astype(BF)


def attend_back(count, listed, owned, proj, q_mark, k_mark, up, out_wide, lse):
    tokens, width = proj.shape
    heads = width // (3 * HEAD_DIM)
    return pl.pallas_call(
        attend_back_kernel,
        grid_spec=pltpu.PrefetchScalarGridSpec(
            num_scalar_prefetch=3,
            grid=(tokens // BQ,),
            in_specs=[
                pl.BlockSpec((BQ, width), lambda i, *_: (i, 0)),
                pl.BlockSpec((BQ, q_mark.shape[1]), lambda i, *_: (i, 0)),
                pl.BlockSpec((BQ, k_mark.shape[1]), lambda i, *_: (i, 0)),
                pl.BlockSpec((BQ, heads * HEAD_DIM), lambda i, *_: (i, 0)),
                pl.BlockSpec((heads, HEAD_DIM, BQ), lambda i, *_: (0, 0, i)),
                pl.BlockSpec((heads, BQ), lambda i, *_: (0, i)),
            ],
            out_specs=whole_block((tokens, width)),
            scratch_shapes=[
                pltpu.VMEM((heads, tokens, LANES), BF),
                pltpu.VMEM((heads * HEAD_DIM, tokens), BF),
                pltpu.VMEM((heads, tokens, HEAD_DIM), BF),
                pltpu.VMEM((heads, BQ, LANES), BF),
                pltpu.VMEM((heads, tokens, HEAD_DIM), F32),
                pltpu.VMEM((heads, tokens, HEAD_DIM), F32),
                pltpu.VMEM((heads, HEAD_DIM, BQ), F32),
            ],
        ),
        out_shape=jax.ShapeDtypeStruct((tokens, width), BF),
        compiler_params=pltpu.CompilerParams(
            dimension_semantics=("arbitrary",), vmem_limit_bytes=44 << 20
        ),
        cost_estimate=pl.CostEstimate(
            flops=heads * tokens * tokens * HEAD_DIM * 10,
            bytes_accessed=heads * tokens * 2048,
            transcendentals=heads * tokens * tokens // 2,
        ),
        name="attend_back",
    )(count, listed, owned, proj, q_mark, k_mark, up, out_wide, lse)


def head_split(matrix, parts):
    rows, cols = matrix.shape
    heads = cols // (parts * HEAD_DIM)
    each = heads // GROUP
    cube = matrix.reshape(rows, parts, heads, HEAD_DIM)
    own = cube[:, :, : each * GROUP].reshape(rows, parts, GROUP, each, HEAD_DIM)
    rest = jnp.broadcast_to(
        cube[:, :, None, each * GROUP :], (rows, parts, GROUP, heads - each * GROUP, HEAD_DIM)
    )
    joined = jnp.concatenate([own, rest], axis=3)
    return jnp.transpose(joined, (2, 0, 1, 3, 4)).reshape(GROUP, rows, -1)


def head_join(shares, parts, heads):
    group, rows, _ = shares.shape
    each = heads // GROUP
    cube = shares.astype(F32).reshape(group, rows, parts, -1, HEAD_DIM)
    own = jnp.transpose(cube[:, :, :, :each], (1, 2, 0, 3, 4)).reshape(
        rows, parts, each * GROUP, HEAD_DIM
    )
    rest = jnp.sum(cube[:, :, :, each:], axis=0)
    return jnp.concatenate([own, rest], axis=2).reshape(rows, -1)


def hidden_split(matrix, unit):
    rows = matrix.shape[0]
    cube = matrix.reshape(rows, -1, GROUP, unit)
    return jnp.transpose(cube, (2, 0, 1, 3)).reshape(GROUP, rows, -1)


def hidden_join(shares, unit):
    group, rows, _ = shares.shape
    cube = shares.reshape(group, rows, -1, unit)
    return jnp.transpose(cube, (1, 2, 0, 3)).reshape(rows, -1)


def exchange(shares):
    return lax.all_to_all(shares, PLANE, split_axis=0, concat_axis=0, tiled=True)


def take(stack, place):
    return lax.dynamic_index_in_dim(stack, place, 0, keepdims=False)


def columns_start(shard, width, split):
    if shard.size % width == 0:
        mine = exchange(split(shard.reshape(-1, width)))
        return mine.reshape(-1, mine.shape[-1])
    return shard


def columns_end(rows, size, width, split, place):
    if size % width == 0:
        return lax.all_gather(rows, TREE, axis=0, tiled=True)
    full = lax.all_gather(rows, EVERY, axis=0, tiled=True).reshape(-1, width)
    return take(split(full), place)


def columns_first(grad, size, width):
    if size % width == 0:
        rows = lax.psum_scatter(grad, TREE, scatter_dimension=0, tiled=True)
        return rows.reshape(GROUP, -1, rows.shape[-1])
    return grad


def columns_second(slots, join, shard_shape, width, place):
    if shard_shape[0] * shard_shape[1] % width == 0:
        return join(slots).astype(F32).reshape(shard_shape)
    spots = jnp.arange(GROUP, dtype=jnp.int32)[:, None, None] == place
    shares = jnp.where(spots, slots[None], jnp.zeros((), BF))
    full = join(shares).astype(BF).reshape(-1, shard_shape[1])
    return lax.psum_scatter(full, EVERY, scatter_dimension=0, tiled=True).astype(F32)


def owner_rows(share, trees):
    t, p, i = (
        lax.broadcasted_iota(jnp.int32, (trees, GROUP, share), dim) for dim in range(3)
    )
    return (t * GROUP + p) * share + i


def slots_out(columns, own, share, place):
    rows = owner_rows(share, lax.axis_size(TREE)) - place * own
    numbers = jnp.arange(own, dtype=jnp.int32)
    pick = jnp.any(rows[..., None] == numbers, axis=0).reshape(-1, own).astype(BF)
    slots = lax.dot_general(
        pick, columns[:, :own], (((1,), (1,)), ((), ())), preferred_element_type=F32
    )
    return slots.astype(BF).reshape(GROUP, share, -1)


def slots_in(slots, own, share, place, padded):
    trees = lax.axis_size(TREE)
    rows = take(jnp.swapaxes(owner_rows(share, trees), 0, 1), place)
    total = jnp.zeros((trees,) + slots.shape[1:], slots.dtype)
    for source in range(GROUP):
        held = (rows >= source * own) & (rows < (source + 1) * own)
        total = jnp.where(held[:, :, None], slots[source][None], total)
    return jnp.pad(total, ((0, 0), (0, padded - share), (0, 0))).reshape(trees * padded, -1)


def on_device(
    tokens,
    cotangent,
    w_qkv,
    w_out,
    w_fc,
    w_proj,
    ln1_gain,
    ln1_bias,
    q_bias,
    v_bias,
    out_bias,
    ln2_gain,
    ln2_bias,
    fc_bias,
    proj_bias,
    seg_lengths,
    parents,
):
    tok_dev, model_width = tokens.shape
    hidden = fc_bias.shape[0]
    flat_cols = w_qkv.shape[1]
    heads = model_width // HEAD_DIM
    each = heads // GROUP
    rest = heads - each * GROUP
    local = each + rest
    tree = lax.axis_index(TREE)
    place = (lax.axis_index("a") * 2 + lax.axis_index("b")) * 2 + lax.axis_index("c")
    device = tree * GROUP + place
    unit = max(1, hidden // lax.axis_size(EVERY))

    starts, ends, reach = tree_tables(take(seg_lengths, tree), take(parents, tree))
    position = jnp.arange(TREE_TOK, dtype=jnp.int32)
    hot = (
        (position[:, None] >= starts[None, :]) & (position[:, None] < ends[None, :])
    ).astype(F32)
    path = jnp.dot(hot, reach, preferred_element_type=F32)
    q_blocks, k_blocks = TREE_TOK // BQ, TREE_TOK // BK
    count, listed = block_lists(hot, path, q_blocks, k_blocks)
    block_numbers = jnp.arange(q_blocks, dtype=jnp.int32)
    turn = q_blocks - 1 - block_numbers
    owner = jnp.where(turn < GROUP, turn, 2 * GROUP - 2 - turn)
    owned = (owner == place).astype(jnp.int32)
    pad = LANES - HEAD_DIM - hot.shape[1]
    k_mark = jnp.pad(hot, ((0, 0), (0, pad))).astype(BF)
    q_mark = jnp.pad((1.0 - path) * NEGATIVE, ((0, 0), (0, pad))).astype(BF)

    residual_in = tokens.astype(F32)
    first_norm, normed_one, inv_one = norm_forward(residual_in, ln1_gain, ln1_bias)
    first_own = first_norm.astype(BF)
    qkv_split, fc_split = partial(head_split, parts=3), partial(hidden_split, unit=unit)
    qkv_rows = columns_start(w_qkv, 3 * model_width, qkv_split)
    w_qkv_l = columns_end(qkv_rows, w_qkv.size, 3 * model_width, qkv_split, place)
    qkv_bias = jnp.concatenate([q_bias, jnp.zeros_like(q_bias), v_bias])
    qkv_bias_l = take(head_split(qkv_bias[None], 3), place)[0]
    first_low, _ = plane_gather(first_own, place)

    two_near = plane_near(after(cotangent, first_low))
    whole_rows = w_out.size % model_width == 0
    ratio = model_width // flat_cols
    w_out_full = lax.all_gather(after(w_out, first_low), EVERY, axis=0, tiled=True)
    w_out_l = jnp.concatenate(
        [
            block_of(w_out_full, place, each * HEAD_DIM * ratio),
            w_out_full[each * GROUP * HEAD_DIM * ratio :],
        ],
        axis=0,
    ).reshape(-1, model_width)
    proj_whole = w_proj.size % model_width == 0
    if proj_whole:
        w_proj_l = lax.all_gather(
            after(w_proj.reshape(-1, model_width), first_low), TREE, axis=0, tiled=True
        )
    else:
        proj_full = lax.all_gather(w_proj, EVERY, axis=0, tiled=True).reshape(hidden, model_width)
        w_proj_l = take(
            jnp.transpose(proj_full.reshape(-1, GROUP, unit, model_width), (1, 0, 2, 3)), place
        ).reshape(-1, model_width)
    fc_bias_l = take(hidden_split(fc_bias[None], unit), place)[0]
    projected = (jnp.dot(first_low, w_qkv_l, preferred_element_type=F32) + qkv_bias_l).astype(BF)

    fc_rows = columns_start(after(w_fc, projected), hidden, fc_split)
    attended, out_wide, lse, tops = attend(count, listed, owned, projected, q_mark, k_mark)
    attended, two_near, fc_rows = lax.optimization_barrier((attended, two_near, fc_rows))
    two_far = plane_far(*two_near)
    w_fc_l = columns_end(fc_rows, w_fc.size, hidden, fc_split, place)
    branch = jnp.dot(attended, w_out_l, preferred_element_type=F32).astype(BF)
    mid_sum, mid_last = plane_scatter(branch, place)
    two_blocks = after((cotangent, *two_near, two_far), *mid_last)
    grad_two = plane_write(two_blocks, [swap(block, "c") for block in two_blocks], place, None)
    middle = residual_in + mid_sum + out_bias

    second_norm, normed_two, inv_two = norm_forward(middle, ln2_gain, ln2_bias)
    second_own = second_norm.astype(BF)
    second_low, _ = plane_gather(second_own, place, branch)
    own_slots = ()
    if whole_rows:
        share = w_out.size // model_width
        own_slots = slots_out(after(attended, second_own), each * HEAD_DIM, share, place)
        own_slots = exchange(after(own_slots, second_low))
    pre_act = jnp.dot(second_low, w_fc_l, preferred_element_type=F32) + fc_bias_l
    activated, gelu_pull = jax.vjp(partial(jax.nn.gelu, approximate=True), pre_act)
    act_low = activated.astype(BF)
    over_cols = lambda left, right: lax.dot_general(
        left, right, (((1,), (1,)), ((), ())), preferred_element_type=F32
    )
    over_rows = lambda left, right: lax.dot_general(
        left, right, (((0,), (0,)), ((), ())), preferred_element_type=F32
    )
    pre_low = gelu_pull(over_cols(grad_two, w_proj_l))[0].astype(BF)
    norm_back = over_cols(pre_low, w_fc_l).astype(BF)
    norm_back, own_slots = lax.optimization_barrier((norm_back, own_slots))
    back_sum, back_last = plane_scatter(norm_back, place)

    grad_out = cotangent.astype(F32)
    proj_bias_grad = jnp.sum(grad_out, axis=0)
    mid_part, ln2_gain_grad, ln2_bias_grad = norm_backward(back_sum, normed_two, inv_two, ln2_gain)
    middle_grad = grad_out + mid_part
    branch_own = middle_grad.astype(BF)
    out_bias_grad = jnp.sum(branch_own.astype(F32), axis=0)

    branch_low, _ = plane_gather(branch_own, place, norm_back)

    fc_low = over_rows(second_low, after(pre_low, branch_own)).astype(BF)
    proj_low = over_rows(after(act_low, branch_own), grad_two).astype(BF)
    branch_two = jnp.dot(
        after(act_low, proj_low), w_proj_l, preferred_element_type=F32
    ).astype(BF)
    attn_back = over_cols(branch_low, w_out_l).astype(BF)
    attn_back = after(attn_back, branch_two)

    two_sum = lax.psum_scatter(
        after(branch_two, branch_low), PLANE, scatter_dimension=0, tiled=True
    )
    fc_rows = columns_first(fc_low, w_fc.size, hidden)
    proj_parts = tree_parts(proj_low) if proj_whole else ()
    qkv_low = attend_back(
        count, listed, owned, projected, q_mark, k_mark, attn_back, out_wide, lse
    )
    qkv_low, fc_rows, proj_parts = lax.optimization_barrier((qkv_low, fc_rows, proj_parts))
    if w_fc.size % hidden == 0:
        fc_rows = exchange(fc_rows)
    first_back = over_cols(qkv_low, w_qkv_l).astype(BF)
    made = []

    def beside(sent):
        made.append(over_rows(first_low, after(qkv_low, two_sum, *sent)).astype(BF))
        return made + [fc_rows]

    in_sum, in_last = plane_scatter(first_back, place, beside)
    qkv_rows = columns_first(made[0], w_qkv.size, 3 * model_width)
    branch_late = after(branch_low, *in_last)
    if whole_rows:
        padded = -(-share // 16) * 16
        out_rows = jnp.dot(
            slots_in(after(own_slots, *in_last), each * HEAD_DIM, share, place, padded),
            branch_late,
            preferred_element_type=F32,
        ).astype(BF)
        out_rows = lax.psum_scatter(
            after(out_rows, qkv_rows), TREE, scatter_dimension=0, tiled=True
        )
        common = over_rows(attended[:, each * HEAD_DIM :], branch_late).astype(BF)
    else:
        out_low = over_rows(attended, branch_late).astype(BF)
        common = jnp.zeros((8, LANES), BF)
    in_part, ln1_gain_grad, ln1_bias_grad = norm_backward(in_sum, normed_one, inv_one, ln1_gain)

    fc_bias_part = jnp.sum(after(pre_low, *in_last).astype(F32), axis=0)
    fc_parts = jnp.zeros((GROUP, hidden // GROUP), F32)
    fc_parts = lax.dynamic_update_slice(fc_parts, fc_bias_part[None], (place, 0))
    fc_parts = hidden_join(fc_parts[:, None], unit)[0]
    column_sums = jnp.sum(after(qkv_low, *in_last).astype(F32), axis=0)
    column_sums = column_sums.reshape(3, local, HEAD_DIM)
    bias_parts = jnp.zeros((3, GROUP, each, HEAD_DIM), F32)
    bias_parts = lax.dynamic_update_slice(
        bias_parts, column_sums[:, None, :each], (0, place, 0, 0)
    )
    bias_parts = jnp.concatenate(
        [bias_parts.reshape(3, each * GROUP, HEAD_DIM), column_sums[:, each:]], axis=1
    ).reshape(3, model_width)
    sums = jnp.concatenate(
        [
            ln1_gain_grad,
            ln1_bias_grad,
            bias_parts[0],
            bias_parts[2],
            out_bias_grad,
            ln2_gain_grad,
            ln2_bias_grad,
            proj_bias_grad,
            fc_parts,
        ]
    )
    top_heads = jnp.max(tops, axis=1)
    spread = jnp.full((GROUP, each), NEGATIVE, F32)
    spread = lax.dynamic_update_slice(spread, top_heads[None, :each], (place, 0))
    spread = jnp.concatenate([spread.reshape(-1), top_heads[each:]])
    is_sum = jnp.arange(sums.shape[0] + heads, dtype=jnp.int32) < sums.shape[0]
    combine = lambda left, right: jnp.where(is_sum, left + right, jnp.maximum(left, right))
    sums = jnp.concatenate([sums, spread])

    whole_qkv = w_qkv.size % (3 * model_width) == 0
    add = lambda left, right: left + right
    combines = [combine, add]
    (common,) = over_trees([common], [add])
    sums, common = over_plane(lax.optimization_barrier((sums, common)), combines)
    if whole_qkv:
        qkv_rows = exchange(after(qkv_rows, in_sum))
    sums, common, qkv_rows = lax.optimization_barrier((sums, common, qkv_rows))
    (sums,) = over_trees([sums], [combine])
    logit_max = sums[-heads:]
    qkv_shard = columns_second(
        qkv_rows, partial(head_join, parts=3, heads=heads), w_qkv.shape, 3 * model_width, place
    )
    fc_shard = columns_second(
        after(fc_rows, sums), partial(hidden_join, unit=unit), w_fc.shape, hidden, place
    )
    if whole_rows:
        rows = device * share + jnp.arange(share, dtype=jnp.int32) - GROUP * each * HEAD_DIM
        numbers = jnp.arange(common.shape[0], dtype=jnp.int32)
        pick = (rows[:, None] == numbers[None, :]).astype(BF)
        out_shard = out_rows[:share].astype(F32) + jnp.dot(
            pick, common, preferred_element_type=F32
        )
        out_shard = out_shard.reshape(w_out.shape)
    else:
        out_zero = jnp.zeros((each * GROUP * HEAD_DIM, model_width), BF)
        out_rows = jnp.concatenate(
            [
                lax.dynamic_update_slice(
                    out_zero, out_low[: each * HEAD_DIM], (place * each * HEAD_DIM, 0)
                ),
                out_low[each * HEAD_DIM :],
            ],
            axis=0,
        ).reshape(-1, flat_cols)
        out_shard = lax.psum_scatter(out_rows, EVERY, scatter_dimension=0, tiled=True).astype(F32)
    if proj_whole:
        proj_shard = sum(part.astype(F32) for part in after(proj_parts, in_sum))
        proj_shard = proj_shard.reshape(w_proj.shape)
    else:
        spots = jnp.arange(GROUP, dtype=jnp.int32)[None, :, None, None] == place
        proj_rows = jnp.where(
            spots, proj_low.reshape(-1, 1, unit, model_width), jnp.zeros((), BF)
        ).reshape(-1, flat_cols)
        proj_shard = lax.psum_scatter(proj_rows, EVERY, scatter_dimension=0, tiled=True).astype(F32)
    input_grad = middle_grad + in_part
    output = (middle + after(two_sum, sums).astype(F32) + proj_bias).astype(BF)

    cut = lambda array, i: array[i * model_width : (i + 1) * model_width]
    small = (
        *(cut(sums, i) for i in range(7)),
        sums[8 * model_width : -heads],
        cut(sums, 7),
    )

    clip_gain = jnp.sqrt(TAU / jnp.maximum(logit_max, TAU))
    rows_dev = w_qkv.shape[0]
    flat_index = (after(device, in_sum) * rows_dev + jnp.arange(rows_dev, dtype=jnp.int32)[:, None]) * flat_cols
    flat_index = flat_index + jnp.arange(flat_cols, dtype=jnp.int32)[None, :]
    column = flat_index % (3 * model_width)
    head_of = column % model_width // HEAD_DIM
    head_numbers = jnp.arange(heads, dtype=jnp.int32)
    head_gain = jnp.sum(
        jnp.where(
            head_of[:, :, None] == head_numbers[None, None, :], clip_gain[None, None, :], 0.0
        ),
        axis=2,
    )
    factor = jnp.where(column < 2 * model_width, head_gain, 1.0)
    clipped = (w_qkv.astype(F32) * factor).astype(BF)
    return (
        output,
        input_grad,
        qkv_shard,
        out_shard,
        fc_shard,
        proj_shard,
        *small,
        logit_max,
        clipped,
    )


def solution(mesh):
    split = Mesh(mesh.devices.reshape(-1, 2, 2, 2), EVERY)
    rows = P(EVERY, None)
    return jax.shard_map(
        on_device,
        mesh=split,
        in_specs=(rows,) * 6 + (P(),) * 11,
        out_specs=(rows,) * 6 + (P(),) * 10 + (rows,),
        check_vma=False,
    )
```
